32 devices in a mesh: ctx: 8 (over y, x, core), head: 4 (over z).
Axes of the slice: x: 2, y: 2, z: 4, core: 2. Of those that a mesh axis runs over, the one named last changes fastest.
Arguments:
- tokens: int32 [2048], P('ctx'), may hold values from 0 to 4
- inputs: bfloat16 [2048, 4096], P('ctx', 'head'), may hold values from -6 to 6
- step_raw: float32 [64, 2048], P('head', 'ctx'), may hold values from -4 to 4
- step_bias: float32 [64], P('head'), may hold values from -1 to 1
- decay_log: float32 [64], P('head'), may hold values from -11 to -3.2
- skip_gain: float32 [64], P('head'), may hold values from 0.5 to 1.5
- bc_table: float32 [2, 5, 128], replicated, may hold values from -0.5 to 0.5
- features: bfloat16 [2048, 1024], P('ctx'), may hold values from -6 to 6
- bc_proj: bfloat16 [2, 1024, 128], replicated, may hold values from -0.01171875 to 0.01171875
- cotangent: bfloat16 [2048, 4096], P('ctx', 'head'), may hold values from -6 to 6
Outputs:
- mixed: bfloat16 [2048, 4096], P('ctx', 'head')
- input_grad: float32 [2048, 4096], P('ctx', 'head')
- step_grad: float32 [64, 2048], P('head', 'ctx')
- table_grad: float32 [2, 5, 128], replicated
- head_grads: float32 [3, 64], P(None, 'head')
- proj_grad: float32 [2, 1024, 128], replicated
The draws below stay inside these ranges and needn't reach their ends.
All inputs are finite; a program needn't handle non-finite values.
Results may differ from the reference program's by a relative error of at most 0.001.
Values sent between devices are 32-bit elements; how exact they have to be, the bound alone decides.
A program may use at most 128 MiB of HBM per device.

```python
import jax
import jax.numpy as jnp
from jax import lax

HEADS = 64
HEAD_DIM = 64
STATE = 128
FEAT = 1024
BLOCK = 128
LENGTH = 2048


def set_ends(array, rng, smallest, top_value):
    extent = array.shape
    place = [jax.random.randint(jax.random.fold_in(rng, axis), (), 0, extent[axis]) for axis in range(len(extent))]
    array = array.at[tuple(place)].set(smallest)
    longest = extent.index(max(extent))
    place[longest] = (place[longest] + 1) % extent[longest]
    return array.at[tuple(place)].set(top_value)


def block_levels(rng, shape, shards, smallest, largest):
    def one(axis_at, parts):
        steps = jax.random.uniform(jax.random.fold_in(jax.random.fold_in(rng, 6), axis_at), (parts,), jnp.float32, smallest / len(shards), largest / len(shards))
        return jnp.repeat(jnp.exp(steps), shape[axis_at] // parts).reshape((-1,) + (1,) * (len(shape) - axis_at - 1))

    loudness = one(*shards[0])
    for cut in shards[1:]:
        loudness = loudness * one(*cut)
    return loudness


def gaussian(own_key, shape, deviation, reach, split=(), held_as=jnp.bfloat16):
    drawn = deviation * jax.random.normal(own_key, shape, jnp.float32)
    if split:
        drawn = drawn * block_levels(own_key, shape, split, -0.22, 0.18)
    return jnp.clip(drawn, -reach, reach).astype(held_as)


def setup_inputs(seed: int = 0) -> dict:
    key_of = jax.random.split(jax.random.key(seed), 11)
    return {
        "tokens": set_ends(jax.random.randint(key_of[0], (LENGTH,), 0, 5), jax.random.fold_in(key_of[0], 1), 0, 4).astype(jnp.int32),
        "inputs": gaussian(key_of[1], (LENGTH, HEADS * HEAD_DIM), 1.0, 6.0, ((0, 8), (1, 4))),
        "step_raw": gaussian(key_of[2], (HEADS, LENGTH), 0.7, 4.0, ((0, 4), (1, 8)), jnp.float32),
        "step_bias": jnp.clip(jax.random.uniform(key_of[3], (HEADS,), jnp.float32, -1.0, 1.0) * block_levels(key_of[3], (HEADS,), ((0, 4),), -0.4, 0.0), -1.0, 1.0),
        "decay_log": jnp.clip(-11.0 + 7.8 * jax.random.uniform(key_of[4], (HEADS,), jnp.float32) ** block_levels(key_of[4], (HEADS,), ((0, 4),), -0.2, 0.2), -11.0, -3.2),
        "skip_gain": jnp.clip(0.5 + 1.0 * jax.random.uniform(key_of[5], (HEADS,), jnp.float32) ** block_levels(key_of[5], (HEADS,), ((0, 4),), -0.2, 0.2), 0.5, 1.5),
        "bc_table": gaussian(key_of[6], (2, 5, STATE), STATE ** -0.5, 0.5, (), jnp.float32),
        "features": gaussian(key_of[7], (LENGTH, FEAT), 1.0, 6.0, ((0, 8),)),
        "bc_proj": gaussian(key_of[8], (2, FEAT, STATE), (2 * FEAT * STATE) ** -0.5, 0.01171875),
        "cotangent": gaussian(key_of[9], (LENGTH, HEADS * HEAD_DIM), 1.0, 6.0, ((0, 8), (1, 4))),
    }


finest = lax.Precision.HIGHEST

def complement_ids(tokens):
    return jnp.where(tokens == 4, 4, 3 - tokens).astype(jnp.int32)

def state_rows(tokens, table, feats, proj):
    onehot = (tokens[:, None] == jnp.arange(5, dtype=jnp.int32)[None, :]).astype(jnp.float32)
    b_rows = jnp.dot(onehot, table[0], precision=finest) + jnp.dot(feats, proj[0], precision=finest)
    c_rows = jnp.dot(onehot, table[1], precision=finest) + jnp.dot(feats, proj[1], precision=finest)
    return (b_rows, c_rows)

def block_scan(values, delta, magnitude, b_rows, c_rows, block):
    length, heads, width = values.shape
    state_dim = b_rows.shape[1]
    count = length // block
    pieces_x = values.reshape(count, block, heads, width)
    pieces_d = delta.reshape(heads, count, block).transpose(1, 0, 2)
    pieces_b = b_rows.reshape(count, block, state_dim)
    pieces_c = c_rows.reshape(count, block, state_dim)
    lower = (jnp.arange(block)[:, None] >= jnp.arange(block)[None, :]).astype(jnp.float32)

    def advance(carry, pieces):
        piece_x, piece_d, piece_b, piece_c = pieces
        cumul = jnp.cumsum(-magnitude[:, None] * piece_d, axis=1)
        driven = piece_x * piece_d.T[:, :, None]
        decay = jnp.exp(jnp.minimum(cumul[:, :, None] - cumul[:, None, :], 0.0)) * lower[None]
        affinity = jnp.dot(piece_c, piece_b.T, precision=finest)
        output = jnp.einsum('hts,shp->thp', decay * affinity[None], driven, precision=finest)
        output = output + jnp.exp(cumul).T[:, :, None] * jnp.einsum('tn,hpn->thp', piece_c, carry, precision=finest)
        weight = jnp.exp(cumul[:, -1:] - cumul)
        carry = jnp.exp(cumul[:, -1])[:, None, None] * carry + jnp.einsum('shp,sn->hpn', driven * weight.T[:, :, None], piece_b, precision=finest)
        return (carry, output)
    start = jnp.zeros((heads, width, state_dim), jnp.float32)
    final, outputs = lax.scan(jax.checkpoint(advance), start, (pieces_x, pieces_d, pieces_b, pieces_c))
    return (outputs.reshape(length, heads, width), final, -magnitude * lax.optimization_barrier(jnp.sum(delta, axis=1)))

def reference(tokens, inputs, step_raw, step_bias, decay_log, skip_gain, bc_table, features, bc_proj, cotangent):
    feats = features.astype(jnp.float32)
    flipped = feats[:, ::-1]

    def forward(values, raw_steps, bias, logs, gain, table, proj):
        delta = jax.nn.softplus(raw_steps + bias[:, None])
        magnitude = jnp.exp(logs)
        tensor = values.reshape(LENGTH, HEADS, HEAD_DIM)
        b_fwd, c_fwd = state_rows(tokens, table, feats, proj)
        b_rev, c_rev = state_rows(complement_ids(tokens), table, flipped, proj)
        fwd_out = block_scan(tensor, delta, magnitude, b_fwd, c_fwd, BLOCK)[0]
        rev_out = block_scan(tensor[::-1], delta[:, ::-1], magnitude, b_rev[::-1], c_rev[::-1], BLOCK)[0][::-1]
        total = fwd_out + rev_out + gain[None, :, None] * tensor
        return total.reshape(LENGTH, HEADS * HEAD_DIM)
    mixed, pullback = jax.vjp(forward, inputs.astype(jnp.float32), step_raw, step_bias, decay_log, skip_gain, bc_table, bc_proj.astype(jnp.float32))
    grads = pullback(cotangent.astype(jnp.float32))
    head_grads = jnp.stack([grads[3], grads[2], grads[4]])
    return (mixed.astype(jnp.bfloat16), grads[0], grads[1], grads[5], head_grads, grads[6])
```

```python
import functools

import jax
import jax.numpy as jnp
from jax import lax
from jax.experimental import pallas as pl
from jax.experimental.pallas import tpu as pltpu
from jax.sharding import PartitionSpec as P

f32, bf16 = jnp.float32, jnp.bfloat16
NN, NT, TN = ((1,), (0,)), ((1,), (1,)), ((0,), (0,))
COMP = (3, 2, 1, 0, 4)
PARAMS = dict(vmem_limit_bytes=50 * 1024 * 1024)


def dg(a, b, dims):
    return lax.dot_general(a, b, (dims, ((), ())), preferred_element_type=f32)


def split(v):
    hi = v.astype(bf16)
    return hi, (v - hi.astype(f32)).astype(bf16)


def mm2(exact, parts, dims):
    return dg(exact, parts[0], dims) + dg(exact, parts[1], dims)


def mm3(a, b, dims):
    return dg(a[0], b[0], dims) + dg(a[0], b[1], dims) + dg(a[1], b[0], dims)


def times_exact(v, exact, dims):
    hi, mid = split(v)
    low = (v - hi.astype(f32) - mid.astype(f32)).astype(bf16)
    return dg(hi, exact, dims) + dg(mid, exact, dims) + dg(low, exact, dims)


def softplus(v):
    return jnp.maximum(v, 0.0) + jnp.log1p(jnp.exp(-jnp.abs(v)))


def iotas(n):
    shape = (n, n)
    return lax.broadcasted_iota(jnp.int32, shape, 0), lax.broadcasted_iota(jnp.int32, shape, 1)


def flip_columns(feats):
    width = feats.shape[1]
    part = 256
    row, col = iotas(part)
    anti = (row + col == part - 1).astype(bf16)
    count = width // part
    return jnp.concatenate(
        [
            dg(feats[:, (count - 1 - k) * part : (count - k) * part], anti, NN).astype(bf16)
            for k in range(count)
        ],
        axis=1,
    )


def prep_kernel(
    tok_ref, x_ref, u_ref, step_ref, bias_ref, dlog_ref, table_ref, feat_ref, proj_ref,
    states_ref, rows_ref, bc_ref, xt_ref, ut_ref, flip_ref, tab, wide_hi, wide_lo,
):
    heads, length = step_ref.shape
    width = x_ref.shape[1] // heads
    delta = softplus(step_ref[...] + bias_ref[...])
    rate = -jnp.exp(dlog_ref[...]) * delta
    row, col = iotas(length)
    cum = times_exact(rate, (row <= col).astype(bf16), NN)
    total = cum[:, length - 1 : length]
    excl = cum - rate
    ef, wf = jnp.exp(cum), jnp.exp(total - cum) * delta
    er, wr = jnp.exp(total - excl), jnp.exp(excl) * delta
    for k, value in enumerate((cum, excl, delta, ef, wf, er, wr, rate)):
        for h in range(heads):
            rows_ref[h, k : k + 1, :] = value[h : h + 1, :]

    tab[...] = jnp.zeros_like(tab)
    tab[0:5, :] = table_ref[0]
    tab[8:13, :] = table_ref[1]
    kinds = lax.broadcasted_iota(jnp.int32, (8, length), 0)
    tok = tok_ref[...]
    hot = (kinds == tok).astype(bf16)
    hot_rev = (kinds == jnp.where(tok == 4, 4, 3 - tok)).astype(bf16)
    feats = feat_ref[...]
    flipped = flip_columns(feats)
    flip_ref[...] = flipped

    def look(onehot, table):
        hi, mid = split(table)
        low = (table - hi.astype(f32) - mid.astype(f32)).astype(bf16)
        return dg(onehot, hi, TN) + dg(onehot, mid, TN) + dg(onehot, low, TN)

    b_fwd = look(hot, tab[0:8, :]) + dg(feats, proj_ref[0], NN)
    c_fwd = look(hot, tab[8:16, :]) + dg(feats, proj_ref[1], NN)
    b_rev = look(hot_rev, tab[0:8, :]) + dg(flipped, proj_ref[0], NN)
    c_rev = look(hot_rev, tab[8:16, :]) + dg(flipped, proj_ref[1], NN)
    for k, value in enumerate((b_fwd, c_fwd, b_rev, c_rev)):
        bc_ref[k] = value

    xt_ref[...] = x_ref[...].astype(f32).T.astype(bf16)
    ut_ref[...] = u_ref[...].astype(f32).T.astype(bf16)
    plan = ((xt_ref, wf, b_fwd), (ut_ref, er, c_rev), (xt_ref, wr, b_rev), (ut_ref, ef, c_fwd))
    for k, (source, scale, right) in enumerate(plan):
        for h in range(heads):
            at = slice(h * width, (h + 1) * width)
            hi, lo = split(source[at, :].astype(f32) * scale[h : h + 1, :])
            wide_hi[at, :] = hi
            wide_lo[at, :] = lo
        states_ref[k] = mm3((wide_hi[...], wide_lo[...]), split(right), NN)


def intra_kernel(
    rows_ref, bc_ref, xt_ref, ut_ref, y_ref, dx_ref, sums_ref, dbc_ref, aff_f, aff_r, total
):
    length = xt_ref.shape[1]
    head = pl.program_id(0)
    row, col = iotas(length)

    @pl.when(head == 0)
    def _():
        b_fwd, c_fwd, b_rev, c_rev = [split(bc_ref[k]) for k in range(4)]
        aff_f[...] = jnp.where(col >= row, mm3(b_fwd, c_fwd, NT), 0.0)
        aff_r[...] = jnp.where(col <= row, mm3(b_rev, c_rev, NT), 0.0)
        total[...] = jnp.zeros_like(total)

    rows = rows_ref[0]
    cols = jnp.concatenate([rows, jnp.zeros((120, length), f32)], axis=0).T
    gap = jnp.where(
        col >= row, rows[0:1, :] - cols[:, 0:1], cols[:, 1:2] - rows[1:2, :]
    )
    decay = jnp.exp(gap) * cols[:, 2:3]
    xt, ut = xt_ref[...], ut_ref[...]
    total[...] += decay * dg(xt, ut, TN)
    v_fwd = split(decay * aff_f[...])
    v_rev = split(decay * aff_r[...])
    y_fwd, y_rev = mm2(xt, v_fwd, NN), mm2(xt, v_rev, NN)
    dx_fwd, dx_rev = mm2(ut, v_fwd, NT), mm2(ut, v_rev, NT)
    y_ref[...] = y_fwd + y_rev
    dx_ref[...] = dx_fwd + dx_rev
    xw, uw = xt.astype(f32), ut.astype(f32)
    sums_ref[0, 0:1, :] = jnp.sum(uw * y_fwd, axis=0, keepdims=True)
    sums_ref[0, 1:2, :] = jnp.sum(uw * y_rev, axis=0, keepdims=True)
    sums_ref[0, 2:3, :] = jnp.sum(xw * dx_fwd, axis=0, keepdims=True)
    sums_ref[0, 3:4, :] = jnp.sum(xw * dx_rev, axis=0, keepdims=True)
    sums_ref[0, 4:5, :] = jnp.sum(xw * uw, axis=0, keepdims=True)

    @pl.when(head == pl.num_programs(0) - 1)
    def _():
        grads = total[...]
        b_fwd, c_fwd, b_rev, c_rev = [split(bc_ref[k]) for k in range(4)]
        g_fwd = split(jnp.where(col >= row, grads, 0.0))
        g_rev = split(jnp.where(col <= row, grads, 0.0))
        dbc_ref[0] = mm3(g_fwd, c_fwd, NN)
        dbc_ref[1] = mm3(g_fwd, b_fwd, TN)
        dbc_ref[2] = mm3(g_rev, c_rev, NN)
        dbc_ref[3] = mm3(g_rev, b_rev, TN)


def finish_kernel(
    tok_ref, step_ref, bias_ref, dlog_ref, gain_ref, rows_ref, sums_ref, bc_ref, dbc_ref,
    xt_ref, ut_ref, y_ref, dx_ref, in_ref, feat_ref, flip_ref,
    mixed_ref, igrad_ref, sgrad_ref, tgrad_ref, hgrad_ref, pgrad_ref,
    inter, wide_hi, wide_lo, heads_scr, const_scr,
):
    heads, length = step_ref.shape
    width = xt_ref.shape[0] // heads
    plan = ((0, 1, 3, ut_ref), (2, 3, 5, ut_ref), (3, 0, 4, xt_ref), (1, 2, 6, xt_ref))
    grads = [None] * 4
    for k, (state, right, scale, source) in enumerate(plan):
        parts = split(in_ref[state])
        inter[k] = mm3(parts, split(bc_ref[right]), NT)
        for h in range(heads):
            at = slice(h * width, (h + 1) * width)
            hi, lo = split(source[at, :].astype(f32) * rows_ref[h, scale : scale + 1, :])
            wide_hi[at, :] = hi
            wide_lo[at, :] = lo
        got = mm3(parts, (wide_hi[...], wide_lo[...]), TN)
        grads[right] = dbc_ref[right] + got.T

    for pair in range(heads // 2):
        ys, dxs = [], []
        for h in (2 * pair, 2 * pair + 1):
            at = slice(h * width, (h + 1) * width)
            xw, uw = xt_ref[at, :].astype(f32), ut_ref[at, :].astype(f32)
            gain = gain_ref[h : h + 1, :]
            y_fwd = inter[0, at, :] * rows_ref[h, 3:4, :]
            y_rev = inter[1, at, :] * rows_ref[h, 5:6, :]
            dx_fwd = inter[2, at, :] * rows_ref[h, 4:5, :]
            dx_rev = inter[3, at, :] * rows_ref[h, 6:7, :]
            ys.append(y_ref[at, :] + y_fwd + y_rev + gain * xw)
            dxs.append(dx_ref[at, :] + dx_fwd + dx_rev + gain * uw)
            a_fwd = jnp.sum(uw * y_fwd, axis=0, keepdims=True)
            a_rev = jnp.sum(uw * y_rev, axis=0, keepdims=True)
            q_fwd = jnp.sum(xw * dx_fwd, axis=0, keepdims=True)
            q_rev = jnp.sum(xw * dx_rev, axis=0, keepdims=True)
            heads_scr[0, h : h + 1, :] = sums_ref[h, 0:1, :] + a_fwd
            heads_scr[1, h : h + 1, :] = sums_ref[h, 1:2, :] + a_rev
            heads_scr[2, h : h + 1, :] = sums_ref[h, 2:3, :] + q_fwd
            heads_scr[3, h : h + 1, :] = sums_ref[h, 3:4, :] + q_rev
            heads_scr[4, h : h + 1, :] = sums_ref[h, 4:5, :]
            heads_scr[5, h : h + 1, :] = q_fwd + q_rev
            cross = in_ref[0, at, :] * in_ref[3, at, :] + in_ref[1, at, :] * in_ref[2, at, :]
            const_scr[h : h + 1, :] = jnp.sum(cross, axis=0, keepdims=True)
        lanes = slice(pair * 2 * width, (pair + 1) * 2 * width)
        mixed_ref[:, lanes] = jnp.concatenate(ys, axis=0).T.astype(bf16)
        igrad_ref[:, lanes] = jnp.concatenate(dxs, axis=0).T

    raw = step_ref[...] + bias_ref[...]
    delta = softplus(raw)
    mag = jnp.exp(dlog_ref[...])
    rate = -mag * delta
    row, col = iotas(length)
    after = (row >= col).astype(bf16)
    before = (row <= col).astype(bf16)
    z_fwd = heads_scr[0] - heads_scr[2]
    z_rev = heads_scr[1] - heads_scr[3]
    decay_all = jnp.exp(jnp.sum(rate, axis=1, keepdims=True))
    const = decay_all * jnp.sum(const_scr[...], axis=1, keepdims=True) + jnp.sum(
        heads_scr[5], axis=1, keepdims=True
    )
    rate_grad = times_exact(z_fwd, after, NN) + times_exact(z_rev, before, NN) + const
    delta_grad = (heads_scr[2] + heads_scr[3]) / delta - mag * rate_grad
    step_grad = delta_grad / (1.0 + jnp.exp(-raw))
    sgrad_ref[...] = step_grad
    hgrad_ref[...] = jnp.zeros_like(hgrad_ref)
    hgrad_ref[:, 0:1] = jnp.sum(rate_grad * rate, axis=1, keepdims=True)
    hgrad_ref[:, 1:2] = jnp.sum(step_grad, axis=1, keepdims=True)
    hgrad_ref[:, 2:3] = jnp.sum(heads_scr[4], axis=1, keepdims=True)

    tok = tok_ref[...]
    kinds = lax.broadcasted_iota(jnp.int32, (8, length), 0)
    hot = (kinds == tok).astype(bf16)
    hot_rev = (kinds == jnp.where(tok == 4, 4, 3 - tok)).astype(bf16)
    parts = [split(g) for g in grads]
    for k in range(2):
        fwd, rev = parts[k], parts[2 + k]
        tgrad_ref[k] = (mm2(hot, fwd, NN) + mm2(hot_rev, rev, NN))[0:5, :]
        pgrad_ref[k] = mm2(feat_ref[...], fwd, TN) + mm2(flip_ref[...], rev, TN)


def call(kernel, outs, scratch, cost=None, **kwargs):
    return pl.pallas_call(
        kernel,
        out_shape=[jax.ShapeDtypeStruct(shape, dtype) for shape, dtype in outs],
        scratch_shapes=[pltpu.VMEM(shape, dtype) for shape, dtype in scratch],
        compiler_params=pltpu.CompilerParams(**PARAMS),
        cost_estimate=cost,
        **kwargs,
    )


def scan_gather(states, decays):
    count, mine = lax.axis_size("ctx"), lax.axis_index("ctx")
    pieces = lax.all_gather(states, "ctx")

    def step(j, sums):
        up, down = sums
        back = count - 1 - j
        longer_up = up * decays[j][:, None] + pieces[j, :2]
        longer_down = down * decays[back][:, None] + pieces[back, 2:]
        return jnp.where(j < mine, longer_up, up), jnp.where(back > mine, longer_down, down)

    zero = jnp.zeros_like(states[:2])
    up, down = lax.fori_loop(0, count - 1, step, (zero, zero))
    return jnp.concatenate([up, down], axis=0)


def scan_pairs(states, decays):
    count, mine = lax.axis_size("ctx"), lax.axis_index("ctx")
    core, pair = mine % 2, mine // 2
    pairs = count // 2
    half = states.shape[1] // 2
    swap = [(i, i ^ 1) for i in range(count)]
    halves = states.reshape(4, 2, half, states.shape[2])
    first = core == 0
    own = jnp.where(first, halves[:, 0], halves[:, 1])
    got = lax.ppermute(jnp.where(first, halves[:, 1], halves[:, 0]), "ctx", swap)
    low, high = jnp.where(first, own, got), jnp.where(first, got, own)
    decays = lax.dynamic_slice_in_dim(decays, core * half, half, 1)
    by_pair = decays.reshape(pairs, 2, half)
    both = by_pair[:, 0] * by_pair[:, 1]
    dec_low = lax.dynamic_index_in_dim(by_pair[:, 0], pair, 0, False)[:, None]
    dec_high = lax.dynamic_index_in_dim(by_pair[:, 1], pair, 0, False)[:, None]
    up = low[:2] * dec_high + high[:2]
    down = high[2:] * dec_low + low[2:]
    index = jnp.arange(pairs)[:, None]
    sum_up, sum_down = 0.0, 0.0
    for k in range(1, pairs):
        other = pair ^ k
        moves = [(i, i ^ (2 * k)) for i in range(count)]
        piece = lax.ppermute(jnp.where(other > pair, up, down), "ctx", moves)
        between = (index > jnp.minimum(pair, other)) & (index < jnp.maximum(pair, other))
        factor = jnp.prod(jnp.where(between, both, 1.0), axis=0)[:, None]
        sum_up += piece * jnp.where(other < pair, factor, 0.0)
        sum_down += piece * jnp.where(other > pair, factor, 0.0)
    for_low = jnp.concatenate([sum_up, sum_down * dec_high + high[2:]], axis=0)
    for_high = jnp.concatenate([sum_up * dec_low + low[:2], sum_down], axis=0)
    keep = jnp.where(first, for_low, for_high)
    other_half = lax.ppermute(jnp.where(first, for_high, for_low), "ctx", swap)
    return jnp.concatenate(
        [jnp.where(first, keep, other_half), jnp.where(first, other_half, keep)], axis=1
    )


def body(
    tokens, inputs, step_raw, step_bias, decay_log, skip_gain, bc_table, features, bc_proj, cotangent
):
    heads, length = step_raw.shape
    wide = inputs.shape[1]
    width = wide // heads
    feat, state = bc_proj.shape[1:]
    tok = tokens.reshape(1, length)
    bias, logs, gain = (v.reshape(heads, 1) for v in (step_bias, decay_log, skip_gain))
    totals = -jnp.exp(decay_log) * jnp.sum(jax.nn.softplus(step_raw + bias), axis=1)
    decays = jnp.exp(jnp.repeat(lax.all_gather(totals, "ctx"), width, axis=1))

    states, rows, bc, xt, ut, flipped = call(
        prep_kernel,
        [
            ((4, wide, state), f32),
            ((heads, 8, length), f32),
            ((4, length, state), f32),
            ((wide, length), bf16),
            ((wide, length), bf16),
            ((length, feat), bf16),
        ],
        [((16, state), f32), ((wide, length), bf16), ((wide, length), bf16)],
    )(tok, inputs, cotangent, step_raw, bias, logs, bc_table, features, bc_proj)

    count = lax.axis_size("ctx")
    paired = count <= 16 and count & (count - 1) == 0 and count > 2 and heads % 2 == 0
    incoming = (scan_pairs if paired else scan_gather)(states, decays)

    per_head = pl.BlockSpec((width, length), lambda h: (h, 0))
    per_rows = pl.BlockSpec((1, 8, length), lambda h: (h, 0, 0))
    whole = pl.BlockSpec((4, length, state), lambda h: (0, 0, 0))
    y, dx, sums, dbc = call(
        intra_kernel,
        [
            ((wide, length), f32),
            ((wide, length), f32),
            ((heads, 8, length), f32),
            ((4, length, state), f32),
        ],
        [((length, length), f32)] * 3,
        pl.CostEstimate(
            flops=heads * length * length * width * 18,
            bytes_accessed=wide * length * 12,
            transcendentals=heads * length * length,
        ),
        grid=(heads,),
        in_specs=[per_rows, whole, per_head, per_head],
        out_specs=[per_head, per_head, per_rows, whole],
    )(rows, bc, xt, ut)

    mixed, input_grad, step_grad, table_local, head_local, proj_local = call(
        finish_kernel,
        [
            ((length, wide), bf16),
            ((length, wide), f32),
            ((heads, length), f32),
            ((2, 5, state), f32),
            ((heads, 128), f32),
            ((2, feat, state), f32),
        ],
        [
            ((4, wide, length), f32),
            ((wide, length), bf16),
            ((wide, length), bf16),
            ((6, heads, length), f32),
            ((heads, state), f32),
        ],
    )(
        tok, step_raw, bias, logs, gain, rows, sums, bc, dbc, xt, ut, y, dx, incoming, features, flipped
    )
    table_grad, proj_grad = lax.psum((table_local, proj_local), ("ctx", "head"))
    head_grads = lax.psum(head_local[:, :3].T, "ctx")
    return mixed, input_grad, step_grad, table_grad, head_grads, proj_grad


def solution(mesh):
    in_specs = (
        P("ctx"),
        P("ctx", "head"),
        P("head", "ctx"),
        P("head"),
        P("head"),
        P("head"),
        P(),
        P("ctx", None),
        P(),
        P("ctx", "head"),
    )
    out_specs = (P("ctx", "head"), P("ctx", "head"), P("head", "ctx"), P(), P(None, "head"), P())
    return jax.shard_map(body, mesh=mesh, in_specs=in_specs, out_specs=out_specs, check_vma=False)
```

```python
import functools

import jax
import jax.numpy as jnp
from jax import lax
from jax.experimental import pallas as pl
from jax.experimental.pallas import tpu as pltpu
from jax.sharding import PartitionSpec as P

f32, bf16 = jnp.float32, jnp.bfloat16
NN, NT, TN = ((1,), (0,)), ((1,), (1,)), ((0,), (0,))
COMP = (3, 2, 1, 0, 4)
PARAMS = dict(vmem_limit_bytes=50 * 1024 * 1024)


def dg(a, b, dims):
    return lax.dot_general(a, b, (dims, ((), ())), preferred_element_type=f32)


def split(v):
    hi = v.astype(bf16)
    return hi, (v - hi.astype(f32)).astype(bf16)


def mm2(exact, parts, dims):
    return dg(exact, parts[0], dims) + dg(exact, parts[1], dims)


def mm3(a, b, dims):
    return dg(a[0], b[0], dims) + dg(a[0], b[1], dims) + dg(a[1], b[0], dims)


def times_exact(v, exact, dims):
    hi, mid = split(v)
    low = (v - hi.astype(f32) - mid.astype(f32)).astype(bf16)
    return dg(hi, exact, dims) + dg(mid, exact, dims) + dg(low, exact, dims)


def softplus(v):
    return jnp.maximum(v, 0.0) + jnp.log1p(jnp.exp(-jnp.abs(v)))


def iotas(n):
    shape = (n, n)
    return lax.broadcasted_iota(jnp.int32, shape, 0), lax.broadcasted_iota(jnp.int32, shape, 1)


def flip_columns(feats):
    width = feats.shape[1]
    part = 256
    row, col = iotas(part)
    anti = (row + col == part - 1).astype(bf16)
    count = width // part
    return jnp.concatenate(
        [
            dg(feats[:, (count - 1 - k) * part : (count - k) * part], anti, NN).astype(bf16)
            for k in range(count)
        ],
        axis=1,
    )


def prep_kernel(
    tok_ref, x_ref, u_ref, step_ref, bias_ref, dlog_ref, table_ref, feat_ref, proj_ref,
    states_ref, rows_ref, bc_ref, xt_ref, ut_ref, flip_ref, tab, wide_hi, wide_lo,
):
    heads, length = step_ref.shape
    width = x_ref.shape[1] // heads
    delta = softplus(step_ref[...] + bias_ref[...])
    rate = -jnp.exp(dlog_ref[...]) * delta
    row, col = iotas(length)
    cum = times_exact(rate, (row <= col).astype(bf16), NN)
    total = cum[:, length - 1 : length]
    excl = cum - rate
    ef, wf = jnp.exp(cum), jnp.exp(total - cum) * delta
    er, wr = jnp.exp(total - excl), jnp.exp(excl) * delta
    for k, value in enumerate((cum, excl, delta, ef, wf, er, wr, rate)):
        for h in range(heads):
            rows_ref[h, k : k + 1, :] = value[h : h + 1, :]

    tab[...] = jnp.zeros_like(tab)
    tab[0:5, :] = table_ref[0]
    tab[8:13, :] = table_ref[1]
    kinds = lax.broadcasted_iota(jnp.int32, (8, length), 0)
    tok = tok_ref[...]
    hot = (kinds == tok).astype(bf16)
    hot_rev = (kinds == jnp.where(tok == 4, 4, 3 - tok)).astype(bf16)
    feats = feat_ref[...]
    flipped = flip_columns(feats)
    flip_ref[...] = flipped

    def look(onehot, table):
        hi, mid = split(table)
        low = (table - hi.astype(f32) - mid.astype(f32)).astype(bf16)
        return dg(onehot, hi, TN) + dg(onehot, mid, TN) + dg(onehot, low, TN)

    b_fwd = look(hot, tab[0:8, :]) + dg(feats, proj_ref[0], NN)
    c_fwd = look(hot, tab[8:16, :]) + dg(feats, proj_ref[1], NN)
    b_rev = look(hot_rev, tab[0:8, :]) + dg(flipped, proj_ref[0], NN)
    c_rev = look(hot_rev, tab[8:16, :]) + dg(flipped, proj_ref[1], NN)
    for k, value in enumerate((b_fwd, c_fwd, b_rev, c_rev)):
        bc_ref[k] = value

    xt_ref[...] = x_ref[...].astype(f32).T.astype(bf16)
    ut_ref[...] = u_ref[...].astype(f32).T.astype(bf16)
    plan = ((xt_ref, wf, b_fwd), (ut_ref, er, c_rev), (xt_ref, wr, b_rev), (ut_ref, ef, c_fwd))
    for k, (source, scale, right) in enumerate(plan):
        for h in range(heads):
            at = slice(h * width, (h + 1) * width)
            hi, lo = split(source[at, :].astype(f32) * scale[h : h + 1, :])
            wide_hi[at, :] = hi
            wide_lo[at, :] = lo
        states_ref[k] = mm3((wide_hi[...], wide_lo[...]), split(right), NN)


def intra_kernel(
    rows_ref, bc_ref, xt_ref, ut_ref, y_ref, dx_ref, sums_ref, dbc_ref, aff_f, aff_r, total
):
    length = xt_ref.shape[1]
    head = pl.program_id(0)
    row, col = iotas(length)

    @pl.when(head == 0)
    def _():
        b_fwd, c_fwd, b_rev, c_rev = [split(bc_ref[k]) for k in range(4)]
        aff_f[...] = jnp.where(col >= row, mm3(b_fwd, c_fwd, NT), 0.0)
        aff_r[...] = jnp.where(col <= row, mm3(b_rev, c_rev, NT), 0.0)
        total[...] = jnp.zeros_like(total)

    rows = rows_ref[0]
    cols = jnp.concatenate([rows, jnp.zeros((120, length), f32)], axis=0).T
    gap = jnp.where(
        col >= row, rows[0:1, :] - cols[:, 0:1], cols[:, 1:2] - rows[1:2, :]
    )
    decay = jnp.exp(gap) * cols[:, 2:3]
    xt, ut = xt_ref[...], ut_ref[...]
    total[...] += decay * dg(xt, ut, TN)
    v_fwd = split(decay * aff_f[...])
    v_rev = split(decay * aff_r[...])
    y_fwd, y_rev = mm2(xt, v_fwd, NN), mm2(xt, v_rev, NN)
    dx_fwd, dx_rev = mm2(ut, v_fwd, NT), mm2(ut, v_rev, NT)
    y_ref[...] = y_fwd + y_rev
    dx_ref[...] = dx_fwd + dx_rev
    xw, uw = xt.astype(f32), ut.astype(f32)
    sums_ref[0, 0:1, :] = jnp.sum(uw * y_fwd, axis=0, keepdims=True)
    sums_ref[0, 1:2, :] = jnp.sum(uw * y_rev, axis=0, keepdims=True)
    sums_ref[0, 2:3, :] = jnp.sum(xw * dx_fwd, axis=0, keepdims=True)
    sums_ref[0, 3:4, :] = jnp.sum(xw * dx_rev, axis=0, keepdims=True)
    sums_ref[0, 4:5, :] = jnp.sum(xw * uw, axis=0, keepdims=True)

    @pl.when(head == pl.num_programs(0) - 1)
    def _():
        grads = total[...]
        b_fwd, c_fwd, b_rev, c_rev = [split(bc_ref[k]) for k in range(4)]
        g_fwd = split(jnp.where(col >= row, grads, 0.0))
        g_rev = split(jnp.where(col <= row, grads, 0.0))
        dbc_ref[0] = mm3(g_fwd, c_fwd, NN)
        dbc_ref[1] = mm3(g_fwd, b_fwd, TN)
        dbc_ref[2] = mm3(g_rev, c_rev, NN)
        dbc_ref[3] = mm3(g_rev, b_rev, TN)


def finish_kernel(
    tok_ref, step_ref, bias_ref, dlog_ref, gain_ref, rows_ref, sums_ref, bc_ref, dbc_ref,
    xt_ref, ut_ref, y_ref, dx_ref, in_ref, feat_ref, flip_ref,
    mixed_ref, igrad_ref, sgrad_ref, sum_ref,
    inter, wide_hi, wide_lo, heads_scr, const_scr,
):
    heads, length = step_ref.shape
    width = xt_ref.shape[0] // heads
    plan = ((0, 1, 3, ut_ref), (2, 3, 5, ut_ref), (3, 0, 4, xt_ref), (1, 2, 6, xt_ref))
    grads = [None] * 4
    for k, (state, right, scale, source) in enumerate(plan):
        parts = split(in_ref[state])
        inter[k] = mm3(parts, split(bc_ref[right]), NT)
        for h in range(heads):
            at = slice(h * width, (h + 1) * width)
            hi, lo = split(source[at, :].astype(f32) * rows_ref[h, scale : scale + 1, :])
            wide_hi[at, :] = hi
            wide_lo[at, :] = lo
        got = mm3(parts, (wide_hi[...], wide_lo[...]), TN)
        grads[right] = dbc_ref[right] + got.T

    for pair in range(heads // 2):
        ys, dxs = [], []
        for h in (2 * pair, 2 * pair + 1):
            at = slice(h * width, (h + 1) * width)
            xw, uw = xt_ref[at, :].astype(f32), ut_ref[at, :].astype(f32)
            gain = gain_ref[h : h + 1, :]
            y_fwd = inter[0, at, :] * rows_ref[h, 3:4, :]
            y_rev = inter[1, at, :] * rows_ref[h, 5:6, :]
            dx_fwd = inter[2, at, :] * rows_ref[h, 4:5, :]
            dx_rev = inter[3, at, :] * rows_ref[h, 6:7, :]
            ys.append(y_ref[at, :] + y_fwd + y_rev + gain * xw)
            dxs.append(dx_ref[at, :] + dx_fwd + dx_rev + gain * uw)
            a_fwd = jnp.sum(uw * y_fwd, axis=0, keepdims=True)
            a_rev = jnp.sum(uw * y_rev, axis=0, keepdims=True)
            q_fwd = jnp.sum(xw * dx_fwd, axis=0, keepdims=True)
            q_rev = jnp.sum(xw * dx_rev, axis=0, keepdims=True)
            heads_scr[0, h : h + 1, :] = sums_ref[h, 0:1, :] + a_fwd
            heads_scr[1, h : h + 1, :] = sums_ref[h, 1:2, :] + a_rev
            heads_scr[2, h : h + 1, :] = sums_ref[h, 2:3, :] + q_fwd
            heads_scr[3, h : h + 1, :] = sums_ref[h, 3:4, :] + q_rev
            heads_scr[4, h : h + 1, :] = sums_ref[h, 4:5, :]
            heads_scr[5, h : h + 1, :] = q_fwd + q_rev
            cross = in_ref[0, at, :] * in_ref[3, at, :] + in_ref[1, at, :] * in_ref[2, at, :]
            const_scr[h : h + 1, :] = jnp.sum(cross, axis=0, keepdims=True)
        lanes = slice(pair * 2 * width, (pair + 1) * 2 * width)
        mixed_ref[:, lanes] = jnp.concatenate(ys, axis=0).T.astype(bf16)
        igrad_ref[:, lanes] = jnp.concatenate(dxs, axis=0).T

    raw = step_ref[...] + bias_ref[...]
    delta = softplus(raw)
    mag = jnp.exp(dlog_ref[...])
    rate = -mag * delta
    row, col = iotas(length)
    after = (row >= col).astype(bf16)
    before = (row <= col).astype(bf16)
    z_fwd = heads_scr[0] - heads_scr[2]
    z_rev = heads_scr[1] - heads_scr[3]
    decay_all = jnp.exp(jnp.sum(rate, axis=1, keepdims=True))
    const = decay_all * jnp.sum(const_scr[...], axis=1, keepdims=True) + jnp.sum(
        heads_scr[5], axis=1, keepdims=True
    )
    rate_grad = times_exact(z_fwd, after, NN) + times_exact(z_rev, before, NN) + const
    delta_grad = (heads_scr[2] + heads_scr[3]) / delta - mag * rate_grad
    step_grad = delta_grad / (1.0 + jnp.exp(-raw))
    sgrad_ref[...] = step_grad
    feat = feat_ref.shape[1]
    sum_ref[2 * feat :, :] = jnp.zeros((sum_ref.shape[0] - 2 * feat, sum_ref.shape[1]), f32)
    mine = pl.ds(2 * feat + 16 + lax.axis_index("head") * heads, heads)
    sum_ref[mine, 0:1] = jnp.sum(rate_grad * rate, axis=1, keepdims=True)
    sum_ref[mine, 1:2] = jnp.sum(step_grad, axis=1, keepdims=True)
    sum_ref[mine, 2:3] = jnp.sum(heads_scr[4], axis=1, keepdims=True)

    tok = tok_ref[...]
    kinds = lax.broadcasted_iota(jnp.int32, (8, length), 0)
    hot = (kinds == tok).astype(bf16)
    hot_rev = (kinds == jnp.where(tok == 4, 4, 3 - tok)).astype(bf16)
    parts = [split(g) for g in grads]
    for k in range(2):
        fwd, rev = parts[k], parts[2 + k]
        at = 2 * feat + 5 * k
        sum_ref[at : at + 5, :] = (mm2(hot, fwd, NN) + mm2(hot_rev, rev, NN))[0:5, :]
        sum_ref[k * feat : (k + 1) * feat, :] = mm2(feat_ref[...], fwd, TN) + mm2(
            flip_ref[...], rev, TN
        )


def remote(src, dst, send, recv, ctx, head):
    return pltpu.make_async_remote_copy(
        src_ref=src,
        dst_ref=dst,
        send_sem=send,
        recv_sem=recv,
        device_id=(ctx, head),
        device_id_type=pl.DeviceIdType.MESH,
    )


def greet(peers):
    barrier = pltpu.get_barrier_semaphore()
    for peer in peers:
        pl.semaphore_signal(
            barrier, inc=1, device_id=peer, device_id_type=pl.DeviceIdType.MESH
        )
    pl.semaphore_wait(barrier, len(peers))


def reduce_kernel(
    part_ref, proj_ref, table_ref, heads_ref, out, acc, got1, got2, got3, gotz, send, recv, sendz, recvz
):
    ctx, head = lax.axis_index("ctx"), lax.axis_index("head")
    bits = (ctx % 2, (ctx // 2) % 2, ctx // 4)
    partners = [ctx + (1 - 2 * bit) * stride for bit, stride in zip(bits, (1, 2, 4))]
    others = [lax.rem(head + d, 4) for d in (1, 2, 3)]
    greet([(p, head) for p in partners] + [(ctx, o) for o in others])
    start, size = 0, part_ref.shape[0]
    kept = []
    for i, (bit, partner, got) in enumerate(zip(bits, partners, (got1, got2, got3))):
        size //= 2
        keep = pl.ds(pl.multiple_of(start + bit * size, 8), size)
        give = pl.ds(pl.multiple_of(start + (1 - bit) * size, 8), size)
        source = part_ref if i == 0 else acc
        copy = remote(source.at[give], got, send.at[i], recv.at[i], partner, head)
        copy.start()
        copy.wait()
        acc[keep, :] = source[keep, :] + got[...]
        kept.append(keep)
        start = start + bit * size
    size //= 4
    quarter = lambda z: pl.ds(pl.multiple_of(start + z * size, 8), size)
    copies = [
        remote(acc.at[quarter(o)], gotz.at[d], sendz.at[d], recvz.at[d], ctx, o)
        for d, o in enumerate(others)
    ]
    for copy in copies:
        copy.start()
    for copy in copies:
        copy.wait()
    mine = quarter(head)
    out[mine, :] = acc[mine, :] + gotz[0] + gotz[1] + gotz[2]
    copies = [
        remote(out.at[mine], out.at[mine], sendz.at[3 + d], recvz.at[3 + d], ctx, o)
        for d, o in enumerate(others)
    ]
    for copy in copies:
        copy.start()
    for copy in copies:
        copy.wait()
    for i in (2, 1, 0):
        copy = remote(
            out.at[kept[i]], out.at[kept[i]], send.at[3 + i], recv.at[3 + i], partners[i], head
        )
        copy.start()
        copy.wait()
    feat, heads = proj_ref.shape[1], heads_ref.shape[0]
    for k in range(2):
        proj_ref[k] = out[k * feat : (k + 1) * feat, :]
        table_ref[k] = out[2 * feat + 5 * k : 2 * feat + 5 * k + 5, :]
    heads_ref[...] = out[pl.ds(pl.multiple_of(2 * feat + 16 + head * heads, 8), heads), :]


def reduce_all(part, feat, heads):
    rows, state = part.shape
    shapes = [(2, feat, state), (2, 5, state), (heads, state)]
    if lax.axis_size("ctx") == 8 and lax.axis_size("head") == 4 and heads % 8 == 0:
        return pl.pallas_call(
            reduce_kernel,
            out_shape=[jax.ShapeDtypeStruct(shape, f32) for shape in shapes],
            scratch_shapes=[
                pltpu.VMEM((rows // cut, state), f32) for cut in (1, 1, 2, 4, 8)
            ]
            + [pltpu.VMEM((3, rows // 32, state), f32)]
            + [pltpu.SemaphoreType.DMA((6,))] * 4,
            in_specs=[pl.BlockSpec(memory_space=pltpu.VMEM)],
            compiler_params=pltpu.CompilerParams(
                collective_id=0, has_side_effects=True, **PARAMS
            ),
        )(part)
    total = lax.psum(part, ("ctx", "head"))
    at = 2 * feat + 16 + lax.axis_index("head") * heads
    return (
        total[: 2 * feat].reshape(shapes[0]),
        total[2 * feat : 2 * feat + 10].reshape(shapes[1]),
        lax.dynamic_slice_in_dim(total, at, heads, 0),
    )


def call(kernel, outs, scratch, cost=None, **kwargs):
    return pl.pallas_call(
        kernel,
        out_shape=[jax.ShapeDtypeStruct(shape, dtype) for shape, dtype in outs],
        scratch_shapes=[pltpu.VMEM(shape, dtype) for shape, dtype in scratch],
        compiler_params=pltpu.CompilerParams(**PARAMS),
        cost_estimate=cost,
        **kwargs,
    )


def scan_gather(states, decays):
    count, mine = lax.axis_size("ctx"), lax.axis_index("ctx")
    pieces = lax.all_gather(states, "ctx")

    def step(j, sums):
        up, down = sums
        back = count - 1 - j
        longer_up = up * decays[j][:, None] + pieces[j, :2]
        longer_down = down * decays[back][:, None] + pieces[back, 2:]
        return jnp.where(j < mine, longer_up, up), jnp.where(back > mine, longer_down, down)

    zero = jnp.zeros_like(states[:2])
    up, down = lax.fori_loop(0, count - 1, step, (zero, zero))
    return jnp.concatenate([up, down], axis=0)


def scan_pairs(states, decays):
    count, mine = lax.axis_size("ctx"), lax.axis_index("ctx")
    core, pair = mine % 2, mine // 2
    pairs = count // 2
    half = states.shape[1] // 2
    swap = [(i, i ^ 1) for i in range(count)]
    halves = states.reshape(4, 2, half, states.shape[2])
    first = core == 0
    own = jnp.where(first, halves[:, 0], halves[:, 1])
    got = lax.ppermute(jnp.where(first, halves[:, 1], halves[:, 0]), "ctx", swap)
    low, high = jnp.where(first, own, got), jnp.where(first, got, own)
    decays = lax.dynamic_slice_in_dim(decays, core * half, half, 1)
    by_pair = decays.reshape(pairs, 2, half)
    both = by_pair[:, 0] * by_pair[:, 1]
    dec_low = lax.dynamic_index_in_dim(by_pair[:, 0], pair, 0, False)[:, None]
    dec_high = lax.dynamic_index_in_dim(by_pair[:, 1], pair, 0, False)[:, None]
    up = low[:2] * dec_high + high[:2]
    down = high[2:] * dec_low + low[2:]
    index = jnp.arange(pairs)[:, None]
    sum_up, sum_down = 0.0, 0.0
    for k in range(1, pairs):
        other = pair ^ k
        moves = [(i, i ^ (2 * k)) for i in range(count)]
        piece = lax.ppermute(jnp.where(other > pair, up, down), "ctx", moves)
        between = (index > jnp.minimum(pair, other)) & (index < jnp.maximum(pair, other))
        factor = jnp.prod(jnp.where(between, both, 1.0), axis=0)[:, None]
        sum_up += piece * jnp.where(other < pair, factor, 0.0)
        sum_down += piece * jnp.where(other > pair, factor, 0.0)
    for_low = jnp.concatenate([sum_up, sum_down * dec_high + high[2:]], axis=0)
    for_high = jnp.concatenate([sum_up * dec_low + low[:2], sum_down], axis=0)
    keep = jnp.where(first, for_low, for_high)
    other_half = lax.ppermute(jnp.where(first, for_high, for_low), "ctx", swap)
    return jnp.concatenate(
        [jnp.where(first, keep, other_half), jnp.where(first, other_half, keep)], axis=1
    )


def body(
    tokens, inputs, step_raw, step_bias, decay_log, skip_gain, bc_table, features, bc_proj, cotangent
):
    heads, length = step_raw.shape
    wide = inputs.shape[1]
    width = wide // heads
    feat, state = bc_proj.shape[1:]
    tok = tokens.reshape(1, length)
    bias, logs, gain = (v.reshape(heads, 1) for v in (step_bias, decay_log, skip_gain))
    totals = -jnp.exp(decay_log) * jnp.sum(jax.nn.softplus(step_raw + bias), axis=1)
    decays = jnp.exp(jnp.repeat(lax.all_gather(totals, "ctx"), width, axis=1))

    states, rows, bc, xt, ut, flipped = call(
        prep_kernel,
        [
            ((4, wide, state), f32),
            ((heads, 8, length), f32),
            ((4, length, state), f32),
            ((wide, length), bf16),
            ((wide, length), bf16),
            ((length, feat), bf16),
        ],
        [((16, state), f32), ((wide, length), bf16), ((wide, length), bf16)],
    )(tok, inputs, cotangent, step_raw, bias, logs, bc_table, features, bc_proj)

    count = lax.axis_size("ctx")
    paired = count <= 16 and count & (count - 1) == 0 and count > 2 and heads % 2 == 0
    incoming = (scan_pairs if paired else scan_gather)(states, decays)

    per_head = pl.BlockSpec((width, length), lambda h: (h, 0))
    per_rows = pl.BlockSpec((1, 8, length), lambda h: (h, 0, 0))
    whole = pl.BlockSpec((4, length, state), lambda h: (0, 0, 0))
    y, dx, sums, dbc = call(
        intra_kernel,
        [
            ((wide, length), f32),
            ((wide, length), f32),
            ((heads, 8, length), f32),
            ((4, length, state), f32),
        ],
        [((length, length), f32)] * 3,
        pl.CostEstimate(
            flops=heads * length * length * width * 18,
            bytes_accessed=wide * length * 12,
            transcendentals=heads * length * length,
        ),
        grid=(heads,),
        in_specs=[per_rows, whole, per_head, per_head],
        out_specs=[per_head, per_head, per_rows, whole],
    )(rows, bc, xt, ut)

    sum_rows = 2 * feat + 16 + heads * lax.axis_size("head")
    mixed, input_grad, step_grad, local_sums = call(
        finish_kernel,
        [
            ((length, wide), bf16),
            ((length, wide), f32),
            ((heads, length), f32),
            ((pl.cdiv(sum_rows, 256) * 256, state), f32),
        ],
        [
            ((4, wide, length), f32),
            ((wide, length), bf16),
            ((wide, length), bf16),
            ((6, heads, length), f32),
            ((heads, state), f32),
        ],
    )(
        tok, step_raw, bias, logs, gain, rows, sums, bc, dbc, xt, ut, y, dx, incoming, features, flipped
    )
    proj_grad, table_grad, head_sums = reduce_all(local_sums, feat, heads)
    head_grads = head_sums[:, :3].T
    return mixed, input_grad, step_grad, table_grad, head_grads, proj_grad


def solution(mesh):
    in_specs = (
        P("ctx"),
        P("ctx", "head"),
        P("head", "ctx"),
        P("head"),
        P("head"),
        P("head"),
        P(),
        P("ctx", None),
        P(),
        P("ctx", "head"),
    )
    out_specs = (P("ctx", "head"), P("ctx", "head"), P("head", "ctx"), P(), P(None, "head"), P())
    return jax.shard_map(body, mesh=mesh, in_specs=in_specs, out_specs=out_specs, check_vma=False)
```

```python
import functools

import jax
import jax.numpy as jnp
from jax import lax
from jax.experimental import pallas as pl
from jax.experimental.pallas import tpu as pltpu
from jax.sharding import PartitionSpec as P

f32, bf16 = jnp.float32, jnp.bfloat16
NN, NT, TN = ((1,), (0,)), ((1,), (1,)), ((0,), (0,))
COMP = (3, 2, 1, 0, 4)
PARAMS = dict(vmem_limit_bytes=50 * 1024 * 1024)


def dg(a, b, dims):
    return lax.dot_general(a, b, (dims, ((), ())), preferred_element_type=f32)


def split(v):
    hi = v.astype(bf16)
    return hi, (v - hi.astype(f32)).astype(bf16)


def mm2(exact, parts, dims):
    return dg(exact, parts[0], dims) + dg(exact, parts[1], dims)


def mm3(a, b, dims):
    return dg(a[0], b[0], dims) + dg(a[0], b[1], dims) + dg(a[1], b[0], dims)


def times_exact(v, exact, dims):
    hi, mid = split(v)
    low = (v - hi.astype(f32) - mid.astype(f32)).astype(bf16)
    return dg(hi, exact, dims) + dg(mid, exact, dims) + dg(low, exact, dims)


def softplus(v):
    return jnp.maximum(v, 0.0) + jnp.log1p(jnp.exp(-jnp.abs(v)))


def iotas(n):
    shape = (n, n)
    return lax.broadcasted_iota(jnp.int32, shape, 0), lax.broadcasted_iota(jnp.int32, shape, 1)


def flip_columns(feats):
    width = feats.shape[1]
    part = 256
    row, col = iotas(part)
    anti = (row + col == part - 1).astype(bf16)
    count = width // part
    return jnp.concatenate(
        [
            dg(feats[:, (count - 1 - k) * part : (count - k) * part], anti, NN).astype(bf16)
            for k in range(count)
        ],
        axis=1,
    )


def prep_kernel(
    tok_ref, x_ref, u_ref, step_ref, bias_ref, dlog_ref, table_ref, feat_ref, proj_ref,
    states_ref, rows_ref, bc_ref, xt_ref, ut_ref, flip_ref, dec_ref, tab, wide_hi, wide_lo,
):
    heads, length = step_ref.shape
    width = x_ref.shape[1] // heads
    delta = softplus(step_ref[...] + bias_ref[...])
    rate = -jnp.exp(dlog_ref[...]) * delta
    row, col = iotas(length)
    cum = times_exact(rate, (row <= col).astype(bf16), NN)
    total = cum[:, length - 1 : length]
    excl = cum - rate
    dec_ref[...] = jnp.broadcast_to(jnp.exp(total), dec_ref.shape)
    ef, wf = jnp.exp(cum), jnp.exp(total - cum) * delta
    er, wr = jnp.exp(total - excl), jnp.exp(excl) * delta
    for k, value in enumerate((cum, excl, delta, ef, wf, er, wr, rate)):
        for h in range(heads):
            rows_ref[h, k : k + 1, :] = value[h : h + 1, :]

    tab[...] = jnp.zeros_like(tab)
    tab[0:5, :] = table_ref[0]
    tab[8:13, :] = table_ref[1]
    kinds = lax.broadcasted_iota(jnp.int32, (8, length), 0)
    tok = tok_ref[...]
    hot = (kinds == tok).astype(bf16)
    hot_rev = (kinds == jnp.where(tok == 4, 4, 3 - tok)).astype(bf16)
    feats = feat_ref[...]
    flipped = flip_columns(feats)
    flip_ref[...] = flipped

    def look(onehot, table):
        hi, mid = split(table)
        low = (table - hi.astype(f32) - mid.astype(f32)).astype(bf16)
        return dg(onehot, hi, TN) + dg(onehot, mid, TN) + dg(onehot, low, TN)

    b_fwd = look(hot, tab[0:8, :]) + dg(feats, proj_ref[0], NN)
    c_fwd = look(hot, tab[8:16, :]) + dg(feats, proj_ref[1], NN)
    b_rev = look(hot_rev, tab[0:8, :]) + dg(flipped, proj_ref[0], NN)
    c_rev = look(hot_rev, tab[8:16, :]) + dg(flipped, proj_ref[1], NN)
    for k, value in enumerate((b_fwd, c_fwd, b_rev, c_rev)):
        bc_ref[k] = value

    xt_ref[...] = x_ref[...].astype(f32).T.astype(bf16)
    ut_ref[...] = u_ref[...].astype(f32).T.astype(bf16)
    plan = ((xt_ref, wf, b_fwd), (ut_ref, er, c_rev), (xt_ref, wr, b_rev), (ut_ref, ef, c_fwd))
    for k, (source, scale, right) in enumerate(plan):
        for h in range(heads):
            at = slice(h * width, (h + 1) * width)
            hi, lo = split(source[at, :].astype(f32) * scale[h : h + 1, :])
            wide_hi[at, :] = hi
            wide_lo[at, :] = lo
        states_ref[k] = mm3((wide_hi[...], wide_lo[...]), split(right), NN)


def exchange_peers():
    ctx, head = lax.axis_index("ctx"), lax.axis_index("head")
    core, pair = ctx % 2, ctx // 2
    x, y = pair % 2, pair // 2
    moves = (1 - 2 * x, 2 - 4 * y, 3 - 2 * x - 4 * y)
    higher = (1 - x, 1 - y, 1 - y)
    return ctx, head, core, pair, moves, higher


def exchange_copies(states_ref, dec_ref, decs, own, got, totals, pieces, inc, send, recv, local):
    ctx, head, core, pair, moves, higher = exchange_peers()
    half = own.shape[1]
    partner = ctx + 1 - 2 * core
    keep = pl.ds(pl.multiple_of(core * half, 8), half)
    give = pl.ds(pl.multiple_of((1 - core) * half, 8), half)
    load = lambda: pltpu.make_async_copy(states_ref.at[:, keep], own, local)
    swap = lambda: remote(states_ref.at[:, give], got, send.at[0], recv.at[0], partner, head)
    chips = lambda: [
        remote(
            totals.at[pl.ds(2 * (1 - up), 2)], pieces.at[k], send.at[1 + k], recv.at[1 + k],
            ctx + 2 * move, head,
        )
        for k, (move, up) in enumerate(zip(moves, higher))
    ]
    back = lambda: remote(totals, inc.at[:, keep], send.at[4], recv.at[4], partner, head)
    rates = lambda: [
        remote(
            decs.at[ctx], decs.at[ctx], send.at[4 + d], recv.at[4 + d],
            lax.rem(ctx + d, 8), head,
        )
        for d in range(1, 8)
    ]
    return load, swap, chips, back, rates


def exchange(states_ref, dec_ref, out_ref, decs, own, got, totals, pieces, inc, send, recv, local):
    refs = (states_ref, dec_ref, decs, own, got, totals, pieces, inc, send, recv, local)
    ctx, head, core, pair, moves, higher = exchange_peers()
    step, last = pl.program_id(0), pl.num_programs(0) - 1
    heads = dec_ref.shape[0] // 2
    width = own.shape[1] // heads
    first = core == 0

    def decay(device, h):
        return decs[device, pl.ds(core * heads + h, 1), :]

    @pl.when(step == 0)
    def _():
        load, swap, _, _, rates = exchange_copies(*refs)
        greet([(lax.rem(ctx + d, 8), head) for d in range(1, 8)])
        load().start()
        swap().start()
        decs[ctx] = dec_ref[...]
        for copy in rates():
            copy.start()

    @pl.when(step == 3)
    def _():
        load, swap, chips, _, rates = exchange_copies(*refs)
        load().wait()
        for copy in [swap()] + rates():
            copy.wait()
        for h in range(heads):
            at = slice(h * width, (h + 1) * width)
            low, high = decay(2 * pair, h), decay(2 * pair + 1, h)
            totals[0:2, at, :] = own[0:2, at, :] * jnp.where(first, high, 1.0) + got[
                0:2, at, :
            ] * jnp.where(first, 1.0, high)
            totals[2:4, at, :] = own[2:4, at, :] * jnp.where(first, 1.0, low) + got[
                2:4, at, :
            ] * jnp.where(first, low, 1.0)
        for copy in chips():
            copy.start()

    @pl.when(step == last)
    def _():
        _, _, chips, back, _ = exchange_copies(*refs)
        for copy in chips():
            copy.wait()
        keep = lambda h: pl.ds(
            pl.multiple_of(core * heads * width + h * width, 8), width
        )
        one = jnp.where(first, 1.0, 0.0)
        for h in range(heads):
            at = slice(h * width, (h + 1) * width)
            low, high = decay(2 * pair, h), decay(2 * pair + 1, h)
            both = {c: decay(2 * c, h) * decay(2 * c + 1, h) for c in (1, 2)}
            up, down = 0.0, 0.0
            for k, (move, higher_k) in enumerate(zip(moves, higher)):
                other = pair + move
                factor = 1.0
                for c in (1, 2):
                    inside = (c - pair) * (other - c) > 0
                    factor = factor * jnp.where(inside, both[c], 1.0)
                piece = pieces[k, :, at, :]
                up += piece * jnp.where(higher_k == 0, factor, 0.0)
                down += piece * jnp.where(higher_k == 1, factor, 0.0)
            inc[0:2, keep(h), :] = up * jnp.where(first, 1.0, low) + got[0:2, at, :] * (1.0 - one)
            inc[2:4, keep(h), :] = down * jnp.where(first, high, 1.0) + got[2:4, at, :] * one
            totals[0:2, at, :] = up * jnp.where(first, low, 1.0) + own[0:2, at, :] * one
            totals[2:4, at, :] = down * jnp.where(first, 1.0, high) + own[2:4, at, :] * (1.0 - one)
        copy = back()
        copy.start()
        copy.wait()
        out_ref[...] = inc[...]


def intra_exchange_kernel(
    states_ref, dec_ref, rows_ref, bc_ref, xt_ref, ut_ref, y_ref, dx_ref, sums_ref, dbc_ref,
    out_ref, aff_f, aff_r, total, *scratch,
):
    intra_kernel(
        rows_ref, bc_ref, xt_ref, ut_ref, y_ref, dx_ref, sums_ref, dbc_ref, aff_f, aff_r, total,
        exchange_step=lambda: exchange(states_ref, dec_ref, out_ref, *scratch),
    )


def intra_kernel(
    rows_ref, bc_ref, xt_ref, ut_ref, y_ref, dx_ref, sums_ref, dbc_ref, aff_f, aff_r, total,
    exchange_step=None,
):
    length = xt_ref.shape[1]
    head = pl.program_id(0)
    row, col = iotas(length)

    @pl.when(head == 0)
    def _():
        b_fwd, c_fwd, b_rev, c_rev = [split(bc_ref[k]) for k in range(4)]
        aff_f[...] = jnp.where(col >= row, mm3(b_fwd, c_fwd, NT), 0.0)
        aff_r[...] = jnp.where(col <= row, mm3(b_rev, c_rev, NT), 0.0)
        total[...] = jnp.zeros_like(total)

    rows = rows_ref[0]
    cols = jnp.concatenate([rows, jnp.zeros((120, length), f32)], axis=0).T
    gap = jnp.where(
        col >= row, rows[0:1, :] - cols[:, 0:1], cols[:, 1:2] - rows[1:2, :]
    )
    decay = jnp.exp(gap) * cols[:, 2:3]
    xt, ut = xt_ref[...], ut_ref[...]
    total[...] += decay * dg(xt, ut, TN)
    v_fwd = split(decay * aff_f[...])
    v_rev = split(decay * aff_r[...])
    y_fwd, y_rev = mm2(xt, v_fwd, NN), mm2(xt, v_rev, NN)
    dx_fwd, dx_rev = mm2(ut, v_fwd, NT), mm2(ut, v_rev, NT)
    y_ref[...] = y_fwd + y_rev
    dx_ref[...] = dx_fwd + dx_rev
    xw, uw = xt.astype(f32), ut.astype(f32)
    sums_ref[0, 0:1, :] = jnp.sum(uw * y_fwd, axis=0, keepdims=True)
    sums_ref[0, 1:2, :] = jnp.sum(uw * y_rev, axis=0, keepdims=True)
    sums_ref[0, 2:3, :] = jnp.sum(xw * dx_fwd, axis=0, keepdims=True)
    sums_ref[0, 3:4, :] = jnp.sum(xw * dx_rev, axis=0, keepdims=True)
    sums_ref[0, 4:5, :] = jnp.sum(xw * uw, axis=0, keepdims=True)

    @pl.when(head == pl.num_programs(0) - 1)
    def _():
        grads = total[...]
        b_fwd, c_fwd, b_rev, c_rev = [split(bc_ref[k]) for k in range(4)]
        g_fwd = split(jnp.where(col >= row, grads, 0.0))
        g_rev = split(jnp.where(col <= row, grads, 0.0))
        dbc_ref[0] = mm3(g_fwd, c_fwd, NN)
        dbc_ref[1] = mm3(g_fwd, b_fwd, TN)
        dbc_ref[2] = mm3(g_rev, c_rev, NN)
        dbc_ref[3] = mm3(g_rev, b_rev, TN)

    if exchange_step is not None:
        exchange_step()


def finish_kernel(
    tok_ref, step_ref, bias_ref, dlog_ref, gain_ref, rows_ref, sums_ref, bc_ref, dbc_ref,
    xt_ref, ut_ref, y_ref, dx_ref, in_ref, feat_ref, flip_ref,
    mixed_ref, igrad_ref, sgrad_ref, sum_ref,
    inter, wide_hi, wide_lo, heads_scr, const_scr,
):
    heads, length = step_ref.shape
    width = xt_ref.shape[0] // heads
    plan = ((0, 1, 3, ut_ref), (2, 3, 5, ut_ref), (3, 0, 4, xt_ref), (1, 2, 6, xt_ref))
    grads = [None] * 4
    for k, (state, right, scale, source) in enumerate(plan):
        parts = split(in_ref[state])
        inter[k] = mm3(parts, split(bc_ref[right]), NT)
        for h in range(heads):
            at = slice(h * width, (h + 1) * width)
            hi, lo = split(source[at, :].astype(f32) * rows_ref[h, scale : scale + 1, :])
            wide_hi[at, :] = hi
            wide_lo[at, :] = lo
        got = mm3(parts, (wide_hi[...], wide_lo[...]), TN)
        grads[right] = dbc_ref[right] + got.T

    for pair in range(heads // 2):
        ys, dxs = [], []
        for h in (2 * pair, 2 * pair + 1):
            at = slice(h * width, (h + 1) * width)
            xw, uw = xt_ref[at, :].astype(f32), ut_ref[at, :].astype(f32)
            gain = gain_ref[h : h + 1, :]
            y_fwd = inter[0, at, :] * rows_ref[h, 3:4, :]
            y_rev = inter[1, at, :] * rows_ref[h, 5:6, :]
            dx_fwd = inter[2, at, :] * rows_ref[h, 4:5, :]
            dx_rev = inter[3, at, :] * rows_ref[h, 6:7, :]
            ys.append(y_ref[at, :] + y_fwd + y_rev + gain * xw)
            dxs.append(dx_ref[at, :] + dx_fwd + dx_rev + gain * uw)
            a_fwd = jnp.sum(uw * y_fwd, axis=0, keepdims=True)
            a_rev = jnp.sum(uw * y_rev, axis=0, keepdims=True)
            q_fwd = jnp.sum(xw * dx_fwd, axis=0, keepdims=True)
            q_rev = jnp.sum(xw * dx_rev, axis=0, keepdims=True)
            heads_scr[0, h : h + 1, :] = sums_ref[h, 0:1, :] + a_fwd
            heads_scr[1, h : h + 1, :] = sums_ref[h, 1:2, :] + a_rev
            heads_scr[2, h : h + 1, :] = sums_ref[h, 2:3, :] + q_fwd
            heads_scr[3, h : h + 1, :] = sums_ref[h, 3:4, :] + q_rev
            heads_scr[4, h : h + 1, :] = sums_ref[h, 4:5, :]
            heads_scr[5, h : h + 1, :] = q_fwd + q_rev
            cross = in_ref[0, at, :] * in_ref[3, at, :] + in_ref[1, at, :] * in_ref[2, at, :]
            const_scr[h : h + 1, :] = jnp.sum(cross, axis=0, keepdims=True)
        lanes = slice(pair * 2 * width, (pair + 1) * 2 * width)
        mixed_ref[:, lanes] = jnp.concatenate(ys, axis=0).T.astype(bf16)
        igrad_ref[:, lanes] = jnp.concatenate(dxs, axis=0).T

    raw = step_ref[...] + bias_ref[...]
    delta = softplus(raw)
    mag = jnp.exp(dlog_ref[...])
    rate = -mag * delta
    row, col = iotas(length)
    after = (row >= col).astype(bf16)
    before = (row <= col).astype(bf16)
    z_fwd = heads_scr[0] - heads_scr[2]
    z_rev = heads_scr[1] - heads_scr[3]
    decay_all = jnp.exp(jnp.sum(rate, axis=1, keepdims=True))
    const = decay_all * jnp.sum(const_scr[...], axis=1, keepdims=True) + jnp.sum(
        heads_scr[5], axis=1, keepdims=True
    )
    rate_grad = times_exact(z_fwd, after, NN) + times_exact(z_rev, before, NN) + const
    delta_grad = (heads_scr[2] + heads_scr[3]) / delta - mag * rate_grad
    step_grad = delta_grad / (1.0 + jnp.exp(-raw))
    sgrad_ref[...] = step_grad
    feat = feat_ref.shape[1]
    sum_ref[2 * feat :, :] = jnp.zeros((sum_ref.shape[0] - 2 * feat, sum_ref.shape[1]), f32)
    mine = pl.ds(2 * feat + 16 + lax.axis_index("head") * heads, heads)
    sum_ref[mine, 0:1] = jnp.sum(rate_grad * rate, axis=1, keepdims=True)
    sum_ref[mine, 1:2] = jnp.sum(step_grad, axis=1, keepdims=True)
    sum_ref[mine, 2:3] = jnp.sum(heads_scr[4], axis=1, keepdims=True)

    tok = tok_ref[...]
    kinds = lax.broadcasted_iota(jnp.int32, (8, length), 0)
    hot = (kinds == tok).astype(bf16)
    hot_rev = (kinds == jnp.where(tok == 4, 4, 3 - tok)).astype(bf16)
    parts = [split(g) for g in grads]
    for k in range(2):
        fwd, rev = parts[k], parts[2 + k]
        at = 2 * feat + 5 * k
        sum_ref[at : at + 5, :] = (mm2(hot, fwd, NN) + mm2(hot_rev, rev, NN))[0:5, :]
        sum_ref[k * feat : (k + 1) * feat, :] = mm2(feat_ref[...], fwd, TN) + mm2(
            flip_ref[...], rev, TN
        )


def remote(src, dst, send, recv, ctx, head):
    return pltpu.make_async_remote_copy(
        src_ref=src,
        dst_ref=dst,
        send_sem=send,
        recv_sem=recv,
        device_id=(ctx, head),
        device_id_type=pl.DeviceIdType.MESH,
    )


def greet(peers):
    barrier = pltpu.get_barrier_semaphore()
    for peer in peers:
        pl.semaphore_signal(
            barrier, inc=1, device_id=peer, device_id_type=pl.DeviceIdType.MESH
        )
    pl.semaphore_wait(barrier, len(peers))


def reduce_kernel(
    part_ref, proj_ref, table_ref, heads_ref, out, acc, got1, got2, got3, gotz, send, recv, sendz, recvz
):
    ctx, head = lax.axis_index("ctx"), lax.axis_index("head")
    bits = (ctx % 2, (ctx // 2) % 2, ctx // 4)
    partners = [ctx + (1 - 2 * bit) * stride for bit, stride in zip(bits, (1, 2, 4))]
    others = [lax.rem(head + d, 4) for d in (1, 2, 3)]
    greet([(p, head) for p in partners] + [(ctx, o) for o in others])
    start, size = 0, part_ref.shape[0]
    kept = []
    for i, (bit, partner, got) in enumerate(zip(bits, partners, (got1, got2, got3))):
        size //= 2
        keep = pl.ds(pl.multiple_of(start + bit * size, 8), size)
        give = pl.ds(pl.multiple_of(start + (1 - bit) * size, 8), size)
        source = part_ref if i == 0 else acc
        copy = remote(source.at[give], got, send.at[i], recv.at[i], partner, head)
        copy.start()
        copy.wait()
        acc[keep, :] = source[keep, :] + got[...]
        kept.append(keep)
        start = start + bit * size
    size //= 4
    quarter = lambda z: pl.ds(pl.multiple_of(start + z * size, 8), size)
    copies = [
        remote(acc.at[quarter(o)], gotz.at[d], sendz.at[d], recvz.at[d], ctx, o)
        for d, o in enumerate(others)
    ]
    for copy in copies:
        copy.start()
    for copy in copies:
        copy.wait()
    mine = quarter(head)
    out[mine, :] = acc[mine, :] + gotz[0] + gotz[1] + gotz[2]
    copies = [
        remote(out.at[mine], out.at[mine], sendz.at[3 + d], recvz.at[3 + d], ctx, o)
        for d, o in enumerate(others)
    ]
    for copy in copies:
        copy.start()
    for copy in copies:
        copy.wait()
    for i in (2, 1, 0):
        copy = remote(
            out.at[kept[i]], out.at[kept[i]], send.at[3 + i], recv.at[3 + i], partners[i], head
        )
        copy.start()
        copy.wait()
    feat, heads = proj_ref.shape[1], heads_ref.shape[0]
    for k in range(2):
        proj_ref[k] = out[k * feat : (k + 1) * feat, :]
        table_ref[k] = out[2 * feat + 5 * k : 2 * feat + 5 * k + 5, :]
    heads_ref[...] = out[pl.ds(pl.multiple_of(2 * feat + 16 + head * heads, 8), heads), :]


def reduce_all(part, feat, heads):
    rows, state = part.shape
    shapes = [(2, feat, state), (2, 5, state), (heads, state)]
    if lax.axis_size("ctx") == 8 and lax.axis_size("head") == 4 and heads % 8 == 0:
        return pl.pallas_call(
            reduce_kernel,
            out_shape=[jax.ShapeDtypeStruct(shape, f32) for shape in shapes],
            scratch_shapes=[
                pltpu.VMEM((rows // cut, state), f32) for cut in (1, 1, 2, 4, 8)
            ]
            + [pltpu.VMEM((3, rows // 32, state), f32)]
            + [pltpu.SemaphoreType.DMA((6,))] * 4,
            in_specs=[pl.BlockSpec(memory_space=pltpu.VMEM)],
            compiler_params=pltpu.CompilerParams(
                collective_id=0, has_side_effects=True, **PARAMS
            ),
        )(part)
    total = lax.psum(part, ("ctx", "head"))
    at = 2 * feat + 16 + lax.axis_index("head") * heads
    return (
        total[: 2 * feat].reshape(shapes[0]),
        total[2 * feat : 2 * feat + 10].reshape(shapes[1]),
        lax.dynamic_slice_in_dim(total, at, heads, 0),
    )


def call(kernel, outs, scratch, cost=None, **kwargs):
    return pl.pallas_call(
        kernel,
        out_shape=[jax.ShapeDtypeStruct(shape, dtype) for shape, dtype in outs],
        scratch_shapes=[pltpu.VMEM(shape, dtype) for shape, dtype in scratch],
        compiler_params=pltpu.CompilerParams(**PARAMS),
        cost_estimate=cost,
        **kwargs,
    )


def scan_gather(states, decays):
    count, mine = lax.axis_size("ctx"), lax.axis_index("ctx")
    pieces = lax.all_gather(states, "ctx")

    def step(j, sums):
        up, down = sums
        back = count - 1 - j
        longer_up = up * decays[j][:, None] + pieces[j, :2]
        longer_down = down * decays[back][:, None] + pieces[back, 2:]
        return jnp.where(j < mine, longer_up, up), jnp.where(back > mine, longer_down, down)

    zero = jnp.zeros_like(states[:2])
    up, down = lax.fori_loop(0, count - 1, step, (zero, zero))
    return jnp.concatenate([up, down], axis=0)


def body(
    tokens, inputs, step_raw, step_bias, decay_log, skip_gain, bc_table, features, bc_proj, cotangent
):
    heads, length = step_raw.shape
    wide = inputs.shape[1]
    width = wide // heads
    feat, state = bc_proj.shape[1:]
    tok = tokens.reshape(1, length)
    bias, logs, gain = (v.reshape(heads, 1) for v in (step_bias, decay_log, skip_gain))
    states, rows, bc, xt, ut, flipped, decay = call(
        prep_kernel,
        [
            ((4, wide, state), f32),
            ((heads, 8, length), f32),
            ((4, length, state), f32),
            ((wide, length), bf16),
            ((wide, length), bf16),
            ((length, feat), bf16),
            ((heads, state), f32),
        ],
        [((16, state), f32), ((wide, length), bf16), ((wide, length), bf16)],
    )(tok, inputs, cotangent, step_raw, bias, logs, bc_table, features, bc_proj)

    per_head = pl.BlockSpec((width, length), lambda h: (h, 0))
    per_rows = pl.BlockSpec((1, 8, length), lambda h: (h, 0, 0))
    whole = pl.BlockSpec((4, length, state), lambda h: (0, 0, 0))
    full = pl.BlockSpec((4, wide, state), lambda h: (0, 0, 0))
    outs = [
        ((wide, length), f32),
        ((wide, length), f32),
        ((heads, 8, length), f32),
        ((4, length, state), f32),
    ]
    squares = [((length, length), f32)] * 3
    in_specs, out_specs = [per_rows, whole, per_head, per_head], [per_head, per_head, per_rows, whole]
    if lax.axis_size("ctx") == 8 and heads % 16 == 0:
        half = wide // 2
        y, dx, sums, dbc, incoming = pl.pallas_call(
            intra_exchange_kernel,
            grid=(heads,),
            out_shape=[
                jax.ShapeDtypeStruct(*out) for out in outs + [((4, wide, state), f32)]
            ],
            in_specs=[
                pl.BlockSpec(memory_space=pl.ANY),
                pl.BlockSpec((heads, state), lambda h: (0, 0)),
            ]
            + in_specs,
            out_specs=out_specs + [full],
            scratch_shapes=[pltpu.VMEM(*square) for square in squares]
            + [pltpu.VMEM((8, heads, state), f32)]
            + [pltpu.VMEM((4, half, state), f32)] * 3
            + [
                pltpu.VMEM((3, 2, half, state), f32),
                pltpu.VMEM((4, wide, state), f32),
                pltpu.SemaphoreType.DMA((12,)),
                pltpu.SemaphoreType.DMA((12,)),
                pltpu.SemaphoreType.DMA,
            ],
            compiler_params=pltpu.CompilerParams(
                collective_id=1, has_side_effects=True, **PARAMS
            ),
        )(states, decay, rows, bc, xt, ut)
    else:
        decays = jnp.repeat(lax.all_gather(decay[:, 0], "ctx"), width, axis=1)
        incoming = scan_gather(states, decays)
        y, dx, sums, dbc = call(
            intra_kernel,
            outs,
            squares,
            pl.CostEstimate(
                flops=heads * length * length * width * 18,
                bytes_accessed=wide * length * 12,
                transcendentals=heads * length * length,
            ),
            grid=(heads,),
            in_specs=in_specs,
            out_specs=out_specs,
        )(rows, bc, xt, ut)

    sum_rows = 2 * feat + 16 + heads * lax.axis_size("head")
    mixed, input_grad, step_grad, local_sums = call(
        finish_kernel,
        [
            ((length, wide), bf16),
            ((length, wide), f32),
            ((heads, length), f32),
            ((pl.cdiv(sum_rows, 256) * 256, state), f32),
        ],
        [
            ((4, wide, length), f32),
            ((wide, length), bf16),
            ((wide, length), bf16),
            ((6, heads, length), f32),
            ((heads, state), f32),
        ],
    )(
        tok, step_raw, bias, logs, gain, rows, sums, bc, dbc, xt, ut, y, dx, incoming, features, flipped
    )
    proj_grad, table_grad, head_sums = reduce_all(local_sums, feat, heads)
    head_grads = head_sums[:, :3].T
    return mixed, input_grad, step_grad, table_grad, head_grads, proj_grad


def solution(mesh):
    in_specs = (
        P("ctx"),
        P("ctx", "head"),
        P("head", "ctx"),
        P("head"),
        P("head"),
        P("head"),
        P(),
        P("ctx", None),
        P(),
        P("ctx", "head"),
    )
    out_specs = (P("ctx", "head"), P("ctx", "head"), P("head", "ctx"), P(), P(None, "head"), P())
    return jax.shard_map(body, mesh=mesh, in_specs=in_specs, out_specs=out_specs, check_vma=False)
```

```python
import functools

import jax
import jax.numpy as jnp
from jax import lax
from jax.experimental import pallas as pl
from jax.experimental.pallas import tpu as pltpu
from jax.sharding import PartitionSpec as P

f32, bf16 = jnp.float32, jnp.bfloat16
NN, NT, TN = ((1,), (0,)), ((1,), (1,)), ((0,), (0,))
COMP = (3, 2, 1, 0, 4)
PARAMS = dict(vmem_limit_bytes=50 * 1024 * 1024)


def dg(a, b, dims):
    return lax.dot_general(a, b, (dims, ((), ())), preferred_element_type=f32)


def split(v):
    hi = v.astype(bf16)
    return hi, (v - hi.astype(f32)).astype(bf16)


def mm2(exact, parts, dims):
    return dg(exact, parts[0], dims) + dg(exact, parts[1], dims)


def mm3(a, b, dims):
    return dg(a[0], b[0], dims) + dg(a[0], b[1], dims) + dg(a[1], b[0], dims)


def times_exact(v, exact, dims):
    hi, mid = split(v)
    low = (v - hi.astype(f32) - mid.astype(f32)).astype(bf16)
    return dg(hi, exact, dims) + dg(mid, exact, dims) + dg(low, exact, dims)


def softplus(v):
    return jnp.maximum(v, 0.0) + jnp.log1p(jnp.exp(-jnp.abs(v)))


def iotas(n):
    shape = (n, n)
    return lax.broadcasted_iota(jnp.int32, shape, 0), lax.broadcasted_iota(jnp.int32, shape, 1)


def flip_columns(feats):
    width = feats.shape[1]
    part = 256
    row, col = iotas(part)
    anti = (row + col == part - 1).astype(bf16)
    count = width // part
    return jnp.concatenate(
        [
            dg(feats[:, (count - 1 - k) * part : (count - k) * part], anti, NN).astype(bf16)
            for k in range(count)
        ],
        axis=1,
    )


def prep_kernel(
    tok_ref, x_ref, u_ref, step_ref, bias_ref, dlog_ref, table_ref, feat_ref, proj_ref,
    states_ref, rows_ref, bc_ref, xt_ref, ut_ref, flip_ref, dec_ref, tab, wide_hi, wide_lo,
):
    heads, length = step_ref.shape
    width = x_ref.shape[1] // heads
    delta = softplus(step_ref[...] + bias_ref[...])
    rate = -jnp.exp(dlog_ref[...]) * delta
    row, col = iotas(length)
    cum = times_exact(rate, (row <= col).astype(bf16), NN)
    total = cum[:, length - 1 : length]
    excl = cum - rate
    dec_ref[...] = jnp.broadcast_to(jnp.exp(total), dec_ref.shape)
    ef, wf = jnp.exp(cum), jnp.exp(total - cum) * delta
    er, wr = jnp.exp(total - excl), jnp.exp(excl) * delta
    for k, value in enumerate((cum, excl, delta, ef, wf, er, wr, rate)):
        for h in range(heads):
            rows_ref[h, k : k + 1, :] = value[h : h + 1, :]

    tab[...] = jnp.zeros_like(tab)
    tab[0:5, :] = table_ref[0]
    tab[8:13, :] = table_ref[1]
    kinds = lax.broadcasted_iota(jnp.int32, (8, length), 0)
    tok = tok_ref[...]
    hot = (kinds == tok).astype(bf16)
    hot_rev = (kinds == jnp.where(tok == 4, 4, 3 - tok)).astype(bf16)
    feats = feat_ref[...]
    flipped = flip_columns(feats)
    flip_ref[...] = flipped

    def look(onehot, table):
        hi, mid = split(table)
        low = (table - hi.astype(f32) - mid.astype(f32)).astype(bf16)
        return dg(onehot, hi, TN) + dg(onehot, mid, TN) + dg(onehot, low, TN)

    b_fwd = look(hot, tab[0:8, :]) + dg(feats, proj_ref[0], NN)
    c_fwd = look(hot, tab[8:16, :]) + dg(feats, proj_ref[1], NN)
    b_rev = look(hot_rev, tab[0:8, :]) + dg(flipped, proj_ref[0], NN)
    c_rev = look(hot_rev, tab[8:16, :]) + dg(flipped, proj_ref[1], NN)
    for k, value in enumerate((b_fwd, c_fwd, b_rev, c_rev)):
        bc_ref[k] = value

    xt_ref[...] = x_ref[...].astype(f32).T.astype(bf16)
    ut_ref[...] = u_ref[...].astype(f32).T.astype(bf16)
    plan = ((xt_ref, wf, b_fwd), (ut_ref, er, c_rev), (xt_ref, wr, b_rev), (ut_ref, ef, c_fwd))
    for k, (source, scale, right) in enumerate(plan):
        for h in range(heads):
            at = slice(h * width, (h + 1) * width)
            hi, lo = split(source[at, :].astype(f32) * scale[h : h + 1, :])
            wide_hi[at, :] = hi
            wide_lo[at, :] = lo
        states_ref[k] = mm3((wide_hi[...], wide_lo[...]), split(right), NN)


def exchange_peers():
    ctx, head = lax.axis_index("ctx"), lax.axis_index("head")
    core, pair = ctx % 2, ctx // 2
    x, y = pair % 2, pair // 2
    moves = (1 - 2 * x, 2 - 4 * y, 3 - 2 * x - 4 * y)
    higher = (1 - x, 1 - y, 1 - y)
    return ctx, head, core, pair, moves, higher


def exchange_copies(states_ref, dec_ref, decs, own, got, totals, pieces, inc, send, recv, local):
    ctx, head, core, pair, moves, higher = exchange_peers()
    half = own.shape[1]
    partner = ctx + 1 - 2 * core
    keep = pl.ds(pl.multiple_of(core * half, 8), half)
    give = pl.ds(pl.multiple_of((1 - core) * half, 8), half)
    load = lambda: pltpu.make_async_copy(states_ref.at[:, keep], own, local)
    swap = lambda: remote(states_ref.at[:, give], got, send.at[0], recv.at[0], partner, head)
    chips = lambda: [
        remote(
            totals.at[pl.ds(2 * (1 - up), 2)], pieces.at[k], send.at[1 + k], recv.at[1 + k],
            ctx + 2 * move, head,
        )
        for k, (move, up) in enumerate(zip(moves, higher))
    ]
    back = lambda: remote(totals, inc.at[:, keep], send.at[4], recv.at[4], partner, head)
    rates = lambda: [
        remote(
            decs.at[ctx], decs.at[ctx], send.at[4 + d], recv.at[4 + d],
            lax.rem(ctx + d, 8), head,
        )
        for d in range(1, 8)
    ]
    return load, swap, chips, back, rates


def exchange(states_ref, dec_ref, out_ref, decs, own, got, totals, pieces, inc, send, recv, local):
    refs = (states_ref, dec_ref, decs, own, got, totals, pieces, inc, send, recv, local)
    ctx, head, core, pair, moves, higher = exchange_peers()
    step, last = pl.program_id(0), pl.num_programs(0) - 1
    heads = dec_ref.shape[0] // 2
    width = own.shape[1] // heads
    first = core == 0

    def decay(device, h):
        return decs[device, pl.ds(core * heads + h, 1), :]

    @pl.when(step == 0)
    def _():
        load, swap, _, _, rates = exchange_copies(*refs)
        greet([(lax.rem(ctx + d, 8), head) for d in range(1, 8)])
        load().start()
        swap().start()
        decs[ctx] = dec_ref[...]
        for copy in rates():
            copy.start()

    @pl.when(step == 3)
    def _():
        load, swap, chips, _, rates = exchange_copies(*refs)
        load().wait()
        for copy in [swap()] + rates():
            copy.wait()
        for h in range(heads):
            at = slice(h * width, (h + 1) * width)
            low, high = decay(2 * pair, h), decay(2 * pair + 1, h)
            totals[0:2, at, :] = own[0:2, at, :] * jnp.where(first, high, 1.0) + got[
                0:2, at, :
            ] * jnp.where(first, 1.0, high)
            totals[2:4, at, :] = own[2:4, at, :] * jnp.where(first, 1.0, low) + got[
                2:4, at, :
            ] * jnp.where(first, low, 1.0)
        for copy in chips():
            copy.start()

    @pl.when(step == last)
    def _():
        _, _, chips, back, _ = exchange_copies(*refs)
        for copy in chips():
            copy.wait()
        keep = lambda h: pl.ds(
            pl.multiple_of(core * heads * width + h * width, 8), width
        )
        one = jnp.where(first, 1.0, 0.0)
        for h in range(heads):
            at = slice(h * width, (h + 1) * width)
            low, high = decay(2 * pair, h), decay(2 * pair + 1, h)
            both = {c: decay(2 * c, h) * decay(2 * c + 1, h) for c in (1, 2)}
            up, down = 0.0, 0.0
            for k, (move, higher_k) in enumerate(zip(moves, higher)):
                other = pair + move
                factor = 1.0
                for c in (1, 2):
                    inside = (c - pair) * (other - c) > 0
                    factor = factor * jnp.where(inside, both[c], 1.0)
                piece = pieces[k, :, at, :]
                up += piece * jnp.where(higher_k == 0, factor, 0.0)
                down += piece * jnp.where(higher_k == 1, factor, 0.0)
            inc[0:2, keep(h), :] = up * jnp.where(first, 1.0, low) + got[0:2, at, :] * (1.0 - one)
            inc[2:4, keep(h), :] = down * jnp.where(first, high, 1.0) + got[2:4, at, :] * one
            totals[0:2, at, :] = up * jnp.where(first, low, 1.0) + own[0:2, at, :] * one
            totals[2:4, at, :] = down * jnp.where(first, 1.0, high) + own[2:4, at, :] * (1.0 - one)
        copy = back()
        copy.start()
        copy.wait()
        out_ref[...] = inc[...]


def intra_exchange_kernel(
    states_ref, dec_ref, rows_ref, bc_ref, xt_ref, ut_ref, y_ref, dx_ref, sums_ref, dbc_ref,
    out_ref, aff_f, aff_r, total, *scratch,
):
    intra_kernel(
        rows_ref, bc_ref, xt_ref, ut_ref, y_ref, dx_ref, sums_ref, dbc_ref, aff_f, aff_r, total,
        exchange_step=lambda: exchange(states_ref, dec_ref, out_ref, *scratch),
    )


def intra_kernel(
    rows_ref, bc_ref, xt_ref, ut_ref, y_ref, dx_ref, sums_ref, dbc_ref, aff_f, aff_r, total,
    exchange_step=None,
):
    length = xt_ref.shape[1]
    head = pl.program_id(0)
    row, col = iotas(length)

    @pl.when(head == 0)
    def _():
        b_fwd, c_fwd, b_rev, c_rev = [split(bc_ref[k]) for k in range(4)]
        aff_f[...] = jnp.where(col >= row, mm3(b_fwd, c_fwd, NT), 0.0)
        aff_r[...] = jnp.where(col <= row, mm3(b_rev, c_rev, NT), 0.0)
        total[...] = jnp.zeros_like(total)

    rows = rows_ref[0]
    cols = jnp.concatenate([rows, jnp.zeros((120, length), f32)], axis=0).T
    gap = jnp.where(
        col >= row, rows[0:1, :] - cols[:, 0:1], cols[:, 1:2] - rows[1:2, :]
    )
    decay = jnp.exp(gap) * cols[:, 2:3]
    xt, ut = xt_ref[...], ut_ref[...]
    total[...] += decay * dg(xt, ut, TN)
    v_fwd = split(decay * aff_f[...])
    v_rev = split(decay * aff_r[...])
    y_fwd, y_rev = mm2(xt, v_fwd, NN), mm2(xt, v_rev, NN)
    dx_fwd, dx_rev = mm2(ut, v_fwd, NT), mm2(ut, v_rev, NT)
    y_ref[...] = y_fwd + y_rev
    dx_ref[...] = dx_fwd + dx_rev
    xw, uw = xt.astype(f32), ut.astype(f32)
    sums_ref[0, 0:1, :] = jnp.sum(uw * y_fwd, axis=0, keepdims=True)
    sums_ref[0, 1:2, :] = jnp.sum(uw * y_rev, axis=0, keepdims=True)
    sums_ref[0, 2:3, :] = jnp.sum(xw * dx_fwd, axis=0, keepdims=True)
    sums_ref[0, 3:4, :] = jnp.sum(xw * dx_rev, axis=0, keepdims=True)
    sums_ref[0, 4:5, :] = jnp.sum(xw * uw, axis=0, keepdims=True)

    @pl.when(head == pl.num_programs(0) - 1)
    def _():
        grads = total[...]
        b_fwd, c_fwd, b_rev, c_rev = [split(bc_ref[k]) for k in range(4)]
        g_fwd = split(jnp.where(col >= row, grads, 0.0))
        g_rev = split(jnp.where(col <= row, grads, 0.0))
        dbc_ref[0] = mm3(g_fwd, c_fwd, NN)
        dbc_ref[1] = mm3(g_fwd, b_fwd, TN)
        dbc_ref[2] = mm3(g_rev, c_rev, NN)
        dbc_ref[3] = mm3(g_rev, b_rev, TN)

    if exchange_step is not None:
        exchange_step()


def finish_kernel(
    tok_ref, step_ref, bias_ref, dlog_ref, gain_ref, rows_ref, sums_ref, bc_ref, dbc_ref,
    xt_ref, ut_ref, y_ref, dx_ref, in_ref, feat_ref, flip_ref,
    mixed_ref, igrad_ref, sgrad_ref, sum_ref,
    inter, wide_hi, wide_lo, heads_scr, const_scr,
):
    heads, length = step_ref.shape
    width = xt_ref.shape[0] // heads
    plan = ((0, 1, 3, ut_ref), (2, 3, 5, ut_ref), (3, 0, 4, xt_ref), (1, 2, 6, xt_ref))
    grads = [None] * 4
    for k, (state, right, scale, source) in enumerate(plan):
        parts = split(in_ref[state])
        inter[k] = mm3(parts, split(bc_ref[right]), NT)
        for h in range(heads):
            at = slice(h * width, (h + 1) * width)
            hi, lo = split(source[at, :].astype(f32) * rows_ref[h, scale : scale + 1, :])
            wide_hi[at, :] = hi
            wide_lo[at, :] = lo
        got = mm3(parts, (wide_hi[...], wide_lo[...]), TN)
        grads[right] = dbc_ref[right] + got.T

    for pair in range(heads // 2):
        ys, dxs = [], []
        for h in (2 * pair, 2 * pair + 1):
            at = slice(h * width, (h + 1) * width)
            xw, uw = xt_ref[at, :].astype(f32), ut_ref[at, :].astype(f32)
            gain = gain_ref[h : h + 1, :]
            y_fwd = inter[0, at, :] * rows_ref[h, 3:4, :]
            y_rev = inter[1, at, :] * rows_ref[h, 5:6, :]
            dx_fwd = inter[2, at, :] * rows_ref[h, 4:5, :]
            dx_rev = inter[3, at, :] * rows_ref[h, 6:7, :]
            ys.append(y_ref[at, :] + y_fwd + y_rev + gain * xw)
            dxs.append(dx_ref[at, :] + dx_fwd + dx_rev + gain * uw)
            a_fwd = jnp.sum(uw * y_fwd, axis=0, keepdims=True)
            a_rev = jnp.sum(uw * y_rev, axis=0, keepdims=True)
            q_fwd = jnp.sum(xw * dx_fwd, axis=0, keepdims=True)
            q_rev = jnp.sum(xw * dx_rev, axis=0, keepdims=True)
            heads_scr[0, h : h + 1, :] = sums_ref[h, 0:1, :] + a_fwd
            heads_scr[1, h : h + 1, :] = sums_ref[h, 1:2, :] + a_rev
            heads_scr[2, h : h + 1, :] = sums_ref[h, 2:3, :] + q_fwd
            heads_scr[3, h : h + 1, :] = sums_ref[h, 3:4, :] + q_rev
            heads_scr[4, h : h + 1, :] = sums_ref[h, 4:5, :]
            heads_scr[5, h : h + 1, :] = q_fwd + q_rev
            cross = in_ref[0, at, :] * in_ref[3, at, :] + in_ref[1, at, :] * in_ref[2, at, :]
            const_scr[h : h + 1, :] = jnp.sum(cross, axis=0, keepdims=True)
        lanes = slice(pair * 2 * width, (pair + 1) * 2 * width)
        mixed_ref[:, lanes] = jnp.concatenate(ys, axis=0).T.astype(bf16)
        igrad_ref[:, lanes] = jnp.concatenate(dxs, axis=0).T

    raw = step_ref[...] + bias_ref[...]
    delta = softplus(raw)
    mag = jnp.exp(dlog_ref[...])
    rate = -mag * delta
    row, col = iotas(length)
    after = (row >= col).astype(bf16)
    before = (row <= col).astype(bf16)
    z_fwd = heads_scr[0] - heads_scr[2]
    z_rev = heads_scr[1] - heads_scr[3]
    decay_all = jnp.exp(jnp.sum(rate, axis=1, keepdims=True))
    const = decay_all * jnp.sum(const_scr[...], axis=1, keepdims=True) + jnp.sum(
        heads_scr[5], axis=1, keepdims=True
    )
    rate_grad = times_exact(z_fwd, after, NN) + times_exact(z_rev, before, NN) + const
    delta_grad = (heads_scr[2] + heads_scr[3]) / delta - mag * rate_grad
    step_grad = delta_grad / (1.0 + jnp.exp(-raw))
    sgrad_ref[...] = step_grad
    feat = feat_ref.shape[1]
    sum_ref[2 * feat :, :] = jnp.zeros((sum_ref.shape[0] - 2 * feat, sum_ref.shape[1]), f32)
    mine = pl.ds(2 * feat + 16 + lax.axis_index("head") * heads, heads)
    sum_ref[mine, 0:1] = jnp.sum(rate_grad * rate, axis=1, keepdims=True)
    sum_ref[mine, 1:2] = jnp.sum(step_grad, axis=1, keepdims=True)
    sum_ref[mine, 2:3] = jnp.sum(heads_scr[4], axis=1, keepdims=True)

    tok = tok_ref[...]
    kinds = lax.broadcasted_iota(jnp.int32, (8, length), 0)
    hot = (kinds == tok).astype(bf16)
    hot_rev = (kinds == jnp.where(tok == 4, 4, 3 - tok)).astype(bf16)
    parts = [split(g) for g in grads]
    for k in range(2):
        fwd, rev = parts[k], parts[2 + k]
        at = 2 * feat + 5 * k
        sum_ref[at : at + 5, :] = (mm2(hot, fwd, NN) + mm2(hot_rev, rev, NN))[0:5, :]
        sum_ref[k * feat : (k + 1) * feat, :] = mm2(feat_ref[...], fwd, TN) + mm2(
            flip_ref[...], rev, TN
        )


def remote(src, dst, send, recv, ctx, head):
    return pltpu.make_async_remote_copy(
        src_ref=src,
        dst_ref=dst,
        send_sem=send,
        recv_sem=recv,
        device_id=(ctx, head),
        device_id_type=pl.DeviceIdType.MESH,
    )


def greet(peers):
    barrier = pltpu.get_barrier_semaphore()
    for peer in peers:
        pl.semaphore_signal(
            barrier, inc=1, device_id=peer, device_id_type=pl.DeviceIdType.MESH
        )
    pl.semaphore_wait(barrier, len(peers))


def reduce_kernel(
    part_ref, proj_ref, table_ref, heads_ref, out, acc, got1, got2, got3, gotz, send, recv, sendz, recvz
):
    ctx, head = lax.axis_index("ctx"), lax.axis_index("head")
    bits = (ctx % 2, (ctx // 2) % 2, ctx // 4)
    partners = [ctx + (1 - 2 * bit) * stride for bit, stride in zip(bits, (1, 2, 4))]
    others = [lax.rem(head + d, 4) for d in (1, 2, 3)]
    greet([(p, head) for p in partners] + [(ctx, o) for o in others])
    def run(copies):
        for copy in copies:
            copy.start()
        for copy in copies:
            copy.wait()

    def span(start, size):
        return pl.ds(pl.multiple_of(start, 8), size)

    size = part_ref.shape[0] // 2
    base = bits[0] * size
    core_keep = span(base, size)
    core_give = span((1 - bits[0]) * size, size)
    run([remote(part_ref.at[core_give], got1, send.at[0], recv.at[0], partners[0], head)])
    acc[core_keep, :] = part_ref[core_keep, :] + got1[...]
    size //= 2
    starts = [base, base + size]
    orders = ((1, 2), (2, 1))
    kept = []
    for i, got in enumerate((got2, got3)):
        size //= 2
        axes = [order[i] for order in orders]
        keeps = [span(at + bits[axis] * size, size) for at, axis in zip(starts, axes)]
        gives = [span(at + (1 - bits[axis]) * size, size) for at, axis in zip(starts, axes)]
        slots = [1 + 2 * i + s for s in range(2)]
        run(
            [
                remote(acc.at[gives[s]], got.at[s], send.at[slots[s]], recv.at[slots[s]],
                       partners[axes[s]], head)
                for s in range(2)
            ]
        )
        for s in range(2):
            acc[keeps[s], :] = acc[keeps[s], :] + got[s]
        kept.append((keeps, axes))
        starts = [at + bits[axis] * size for at, axis in zip(starts, axes)]
    size //= 4
    both = [(s, d, o) for s in range(2) for d, o in enumerate(others)]
    run(
        [
            remote(acc.at[span(starts[s] + o * size, size)], gotz.at[s, d],
                   sendz.at[3 * s + d], recvz.at[3 * s + d], ctx, o)
            for s, d, o in both
        ]
    )
    mine = [span(at + head * size, size) for at in starts]
    for s in range(2):
        out[mine[s], :] = acc[mine[s], :] + gotz[s, 0] + gotz[s, 1] + gotz[s, 2]
    run(
        [
            remote(out.at[mine[s]], out.at[mine[s]],
                   sendz.at[6 + 3 * s + d], recvz.at[6 + 3 * s + d], ctx, o)
            for s, d, o in both
        ]
    )
    for i in (1, 0):
        keeps, axes = kept[i]
        slots = [5 + 2 * i + s for s in range(2)]
        run(
            [
                remote(out.at[keeps[s]], out.at[keeps[s]], send.at[slots[s]], recv.at[slots[s]],
                       partners[axes[s]], head)
                for s in range(2)
            ]
        )
    run([remote(out.at[core_keep], out.at[core_keep], send.at[9], recv.at[9], partners[0], head)])
    feat, heads = proj_ref.shape[1], heads_ref.shape[0]
    for k in range(2):
        proj_ref[k] = out[k * feat : (k + 1) * feat, :]
        table_ref[k] = out[2 * feat + 5 * k : 2 * feat + 5 * k + 5, :]
    heads_ref[...] = out[pl.ds(pl.multiple_of(2 * feat + 16 + head * heads, 8), heads), :]


def reduce_all(part, feat, heads):
    rows, state = part.shape
    shapes = [(2, feat, state), (2, 5, state), (heads, state)]
    if lax.axis_size("ctx") == 8 and lax.axis_size("head") == 4 and heads % 8 == 0:
        return pl.pallas_call(
            reduce_kernel,
            out_shape=[jax.ShapeDtypeStruct(shape, f32) for shape in shapes],
            scratch_shapes=[
                pltpu.VMEM((rows // cut, state), f32) for cut in (1, 1, 2)
            ]
            + [pltpu.VMEM((2, rows // cut, state), f32) for cut in (8, 16)]
            + [pltpu.VMEM((2, 3, rows // 64, state), f32)]
            + [pltpu.SemaphoreType.DMA((12,))] * 4,
            in_specs=[pl.BlockSpec(memory_space=pltpu.VMEM)],
            compiler_params=pltpu.CompilerParams(
                collective_id=0, has_side_effects=True, **PARAMS
            ),
        )(part)
    total = lax.psum(part, ("ctx", "head"))
    at = 2 * feat + 16 + lax.axis_index("head") * heads
    return (
        total[: 2 * feat].reshape(shapes[0]),
        total[2 * feat : 2 * feat + 10].reshape(shapes[1]),
        lax.dynamic_slice_in_dim(total, at, heads, 0),
    )


def call(kernel, outs, scratch, cost=None, **kwargs):
    return pl.pallas_call(
        kernel,
        out_shape=[jax.ShapeDtypeStruct(shape, dtype) for shape, dtype in outs],
        scratch_shapes=[pltpu.VMEM(shape, dtype) for shape, dtype in scratch],
        compiler_params=pltpu.CompilerParams(**PARAMS),
        cost_estimate=cost,
        **kwargs,
    )


def scan_gather(states, decays):
    count, mine = lax.axis_size("ctx"), lax.axis_index("ctx")
    pieces = lax.all_gather(states, "ctx")

    def step(j, sums):
        up, down = sums
        back = count - 1 - j
        longer_up = up * decays[j][:, None] + pieces[j, :2]
        longer_down = down * decays[back][:, None] + pieces[back, 2:]
        return jnp.where(j < mine, longer_up, up), jnp.where(back > mine, longer_down, down)

    zero = jnp.zeros_like(states[:2])
    up, down = lax.fori_loop(0, count - 1, step, (zero, zero))
    return jnp.concatenate([up, down], axis=0)


def body(
    tokens, inputs, step_raw, step_bias, decay_log, skip_gain, bc_table, features, bc_proj, cotangent
):
    heads, length = step_raw.shape
    wide = inputs.shape[1]
    width = wide // heads
    feat, state = bc_proj.shape[1:]
    tok = tokens.reshape(1, length)
    bias, logs, gain = (v.reshape(heads, 1) for v in (step_bias, decay_log, skip_gain))
    states, rows, bc, xt, ut, flipped, decay = call(
        prep_kernel,
        [
            ((4, wide, state), f32),
            ((heads, 8, length), f32),
            ((4, length, state), f32),
            ((wide, length), bf16),
            ((wide, length), bf16),
            ((length, feat), bf16),
            ((heads, state), f32),
        ],
        [((16, state), f32), ((wide, length), bf16), ((wide, length), bf16)],
    )(tok, inputs, cotangent, step_raw, bias, logs, bc_table, features, bc_proj)

    per_head = pl.BlockSpec((width, length), lambda h: (h, 0))
    per_rows = pl.BlockSpec((1, 8, length), lambda h: (h, 0, 0))
    whole = pl.BlockSpec((4, length, state), lambda h: (0, 0, 0))
    full = pl.BlockSpec((4, wide, state), lambda h: (0, 0, 0))
    outs = [
        ((wide, length), f32),
        ((wide, length), f32),
        ((heads, 8, length), f32),
        ((4, length, state), f32),
    ]
    squares = [((length, length), f32)] * 3
    in_specs, out_specs = [per_rows, whole, per_head, per_head], [per_head, per_head, per_rows, whole]
    if lax.axis_size("ctx") == 8 and heads % 16 == 0:
        half = wide // 2
        y, dx, sums, dbc, incoming = pl.pallas_call(
            intra_exchange_kernel,
            grid=(heads,),
            out_shape=[
                jax.ShapeDtypeStruct(*out) for out in outs + [((4, wide, state), f32)]
            ],
            in_specs=[
                pl.BlockSpec(memory_space=pl.ANY),
                pl.BlockSpec((heads, state), lambda h: (0, 0)),
            ]
            + in_specs,
            out_specs=out_specs + [full],
            scratch_shapes=[pltpu.VMEM(*square) for square in squares]
            + [pltpu.VMEM((8, heads, state), f32)]
            + [pltpu.VMEM((4, half, state), f32)] * 3
            + [
                pltpu.VMEM((3, 2, half, state), f32),
                pltpu.VMEM((4, wide, state), f32),
                pltpu.SemaphoreType.DMA((12,)),
                pltpu.SemaphoreType.DMA((12,)),
                pltpu.SemaphoreType.DMA,
            ],
            compiler_params=pltpu.CompilerParams(
                collective_id=1, has_side_effects=True, **PARAMS
            ),
        )(states, decay, rows, bc, xt, ut)
    else:
        decays = jnp.repeat(lax.all_gather(decay[:, 0], "ctx"), width, axis=1)
        incoming = scan_gather(states, decays)
        y, dx, sums, dbc = call(
            intra_kernel,
            outs,
            squares,
            pl.CostEstimate(
                flops=heads * length * length * width * 18,
                bytes_accessed=wide * length * 12,
                transcendentals=heads * length * length,
            ),
            grid=(heads,),
            in_specs=in_specs,
            out_specs=out_specs,
        )(rows, bc, xt, ut)

    sum_rows = 2 * feat + 16 + heads * lax.axis_size("head")
    mixed, input_grad, step_grad, local_sums = call(
        finish_kernel,
        [
            ((length, wide), bf16),
            ((length, wide), f32),
            ((heads, length), f32),
            ((pl.cdiv(sum_rows, 512) * 512, state), f32),
        ],
        [
            ((4, wide, length), f32),
            ((wide, length), bf16),
            ((wide, length), bf16),
            ((6, heads, length), f32),
            ((heads, state), f32),
        ],
    )(
        tok, step_raw, bias, logs, gain, rows, sums, bc, dbc, xt, ut, y, dx, incoming, features, flipped
    )
    proj_grad, table_grad, head_sums = reduce_all(local_sums, feat, heads)
    head_grads = head_sums[:, :3].T
    return mixed, input_grad, step_grad, table_grad, head_grads, proj_grad


def solution(mesh):
    in_specs = (
        P("ctx"),
        P("ctx", "head"),
        P("head", "ctx"),
        P("head"),
        P("head"),
        P("head"),
        P(),
        P("ctx", None),
        P(),
        P("ctx", "head"),
    )
    out_specs = (P("ctx", "head"), P("ctx", "head"), P("head", "ctx"), P(), P(None, "head"), P())
    return jax.shard_map(body, mesh=mesh, in_specs=in_specs, out_specs=out_specs, check_vma=False)
```
